512 devices in a mesh: dp: 32 (over z, y_lo, core), ctx: 16 (over y_hi, x).
Axes of the slice: x: 4, y: 8 (y_hi: 4, y_lo: 2; y = y_hi * 2 + y_lo), z: 8, core: 2. Of those that a mesh axis runs over, the one named last changes fastest.
Arguments:
- activations: bfloat16 [32, 2048, 2048], P('dp', 'ctx'), may hold values from -8 to 8
- out_grads: bfloat16 [32, 2048, 2048], P('dp', 'ctx'), may hold values from -64 to 64
- segment_ids: int32 [32, 2048], P('dp', 'ctx'), may hold values from -1 to 7, as said below
Outputs:
- weight_grad: float32 [2048, 2048], P('ctx', 'dp')
- clip_factors: float32 [32, 8], P('dp')
The draws below stay inside these ranges and needn't reach their ends.
Inputs may be any that keep to these rules, and one draw needn't show every extreme that they name: `segment_ids`: each sequence holds 8 documents, numbered in order; each occupies one or more whole consecutive blocks of 128 tokens, and -1 (padding) occurs only at the end of a document's last block; every document has at least one token.
All inputs are finite; a program needn't handle non-finite values.
Results may differ from the reference program's by a relative error of at most 0.0016.
Values may be sent and summed in bfloat16 or wider, within the bound.
No kernel may reach another device: no remote copies, remote signals or barrier semaphores. Data moves between devices by JAX's collectives and lax.ppermute only.
A program may use at most 128 MiB of HBM per device.

```python
import jax
import jax.numpy as jnp
from jax import lax

D_IN = 2048
D_OUT = 2048
BLOCK = 128
SEQ = 2048
SEQS = 32
DOCS = 8


pool_factor = 2


def segment_table(key):
    block_count = SEQ // BLOCK

    def one_sequence(seq_key):
        cut_key, pad_key = jax.random.split(seq_key)
        shuffled = jax.random.permutation(cut_key, block_count - 1) + 1
        cuts = jnp.sort(shuffled[:DOCS - 1])
        block_index = jnp.arange(block_count)
        block_doc = jnp.sum(block_index[:, None] >= cuts[None, :], axis=1).astype(jnp.int32)
        next_doc = jnp.concatenate([block_doc[1:], jnp.full((1,), DOCS, jnp.int32)])
        last_block = next_doc != block_doc
        padding = jax.random.randint(pad_key, (block_count,), 0, BLOCK)
        token_block = jnp.arange(SEQ) // BLOCK
        in_block = jnp.arange(SEQ) % BLOCK
        is_padding = last_block[token_block] & (in_block >= BLOCK - padding[token_block])
        return jnp.where(is_padding, -1, block_doc[token_block]).astype(jnp.int32)
    seq_keys = jax.random.split(key, SEQS)
    return jax.vmap(one_sequence)(seq_keys)


def draw_segment_ids(key, part):
    return segment_table(jax.random.fold_in(key, 17))


def atom_table(key):
    pool = pool_factor * BLOCK
    seq_ids = segment_table(jax.random.fold_in(key, 17))
    picks = jax.random.randint(jax.random.fold_in(key, 53), (SEQS, SEQ), 0, pool).astype(jnp.int32)
    return (jnp.maximum(seq_ids, 0) * pool + picks).astype(jnp.int32)


def document_mixture(key, width, basis_tag, noise_tag):
    pool = pool_factor * BLOCK
    atoms = atom_table(key)
    basis_keys = jax.random.split(jax.random.fold_in(key, basis_tag), SEQS)
    noise_keys = jax.random.split(jax.random.fold_in(key, noise_tag), SEQS)
    share = 0.5

    def one_sequence(inputs):
        atom_row, basis_key, noise_key = inputs
        basis = jax.random.normal(basis_key, (DOCS * pool, width), jnp.float32)
        noise = jax.random.truncated_normal(noise_key, -4.0, 4.0, (SEQ, width), jnp.float32)
        shared = jnp.take(basis, atom_row, axis=0)
        return jnp.sqrt(1.0 - share) * noise + jnp.sqrt(share) * shared
    mixed = lax.map(one_sequence, (atoms, basis_keys, noise_keys))
    return (mixed, share)


def draw_activations(key, part):
    mixed, share = document_mixture(key, D_IN, 31, 37)
    return jnp.clip(mixed, -8.0, 8.0).astype(jnp.bfloat16)


def draw_out_grads(key, part):
    mixed, share = document_mixture(key, D_OUT, 41, 43)
    typical = 2.0 * BLOCK
    pool = pool_factor * BLOCK
    spread = 1.0 + typical * share * share / pool
    scale = 600.0 / jnp.sqrt(jnp.float32(D_IN) * jnp.float32(D_OUT) * typical * spread)
    values = mixed * scale
    return jnp.clip(values, -64.0, 64.0).astype(jnp.bfloat16)


def setup_inputs(seed: int = 0) -> dict:
    keys = jax.random.split(jax.random.key(seed), 4)
    activations = draw_activations(jax.random.fold_in(keys[3], 71), 0)
    out_grads = draw_out_grads(jax.random.fold_in(keys[3], 71), 0)
    segment_ids = draw_segment_ids(jax.random.fold_in(keys[3], 71), 0)
    return dict(activations=activations, out_grads=out_grads, segment_ids=segment_ids)


clip_bound = 600.0

def reference(activations, out_grads, segment_ids):
    doc_range = jnp.arange(DOCS, dtype=jnp.int32)

    def one_sequence(grad_total, inputs):
        seq_acts, seq_grads, seq_ids = inputs
        gram_in = jnp.dot(seq_acts, seq_acts.T, preferred_element_type=jnp.float32)
        gram_out = jnp.dot(seq_grads, seq_grads.T, preferred_element_type=jnp.float32)
        same_doc = (seq_ids[:, None] == seq_ids[None, :]) & (seq_ids[:, None] >= 0)
        per_token = lax.optimization_barrier(jnp.sum(jnp.where(same_doc, gram_in * gram_out, jnp.float32(0.0)), axis=1))
        one_hot = (seq_ids[:, None] == doc_range[None, :]).astype(jnp.float32)
        norm_sq = jnp.dot(per_token, one_hot, precision=lax.Precision.HIGHEST)
        clip_factor = clip_bound / jnp.sqrt(jnp.maximum(norm_sq, clip_bound * clip_bound))
        token_clip = jnp.dot(one_hot, clip_factor, precision=lax.Precision.HIGHEST)
        scaled = (seq_grads.astype(jnp.float32) * token_clip[:, None]).astype(jnp.bfloat16)
        partial_grad = lax.dot_general(seq_acts, scaled, (((0,), (0,)), ((), ())), preferred_element_type=jnp.float32)
        return (grad_total + partial_grad, clip_factor)
    start_grad = jnp.zeros((D_IN, D_OUT), jnp.float32)
    weight_grad, clip_factors = lax.scan(one_sequence, start_grad, (activations, out_grads, segment_ids))
    return (weight_grad, clip_factors)
```

```python
import functools

import jax
import jax.numpy as jnp
import numpy as np
from jax import lax
from jax.experimental import pallas as pl
from jax.experimental.pallas import tpu as pltpu
from jax.sharding import Mesh
from jax.sharding import PartitionSpec as P


INTERPRET = False
CLIP = 600.0
BLOCK = 128
COLS = 64
DOCS = 8

AXES = ("zh", "zl", "yl", "c", "yh", "x")


def table(mesh_sizes, axes, to):
    dims = [mesh_sizes[a] for a in axes]
    pairs = []
    for src in range(int(np.prod(dims))):
        at = dict(zip(axes, np.unravel_index(src, dims)))
        dst = to(**at)
        pairs.append((src, int(np.ravel_multi_index([int(dst[a]) for a in axes], dims))))
    return pairs


def to_group(k, zl, yl, c, yh, x):
    j = (yh + k) % 4
    return dict(zl=j // 2, yl=1 - yl, c=j % 2, yh=zl * 2 + c, x=(x + k) % 4)


def prep_kernel(pos, ids_ref, a_ref, g_ref, *rest):
    outs, gt_ref = rest[:4], rest[4]
    x, yh = pos[0], pos[1]
    chunks = g_ref.shape[1] // BLOCK
    kept = ids_ref[...] >= 0
    for n in range(chunks):
        t = g_ref[:, n * BLOCK : (n + 1) * BLOCK].astype(jnp.float32).T
        gt_ref[n * BLOCK : (n + 1) * BLOCK, :] = jnp.where(kept, t, 0.0).astype(jnp.bfloat16)
    for k in range(4):
        i = (x + k) % 4
        j = (yh + k) % 4
        for r in range(4):
            at = pl.multiple_of((r * 4 + i) * BLOCK, BLOCK)
            outs[k][r] = a_ref[:, pl.ds(at, BLOCK)]
        for h in range(chunks // 4):
            for half in range(2):
                at = pl.multiple_of(((h * 2 + j // 2) * 2 + half) * BLOCK + (j % 2) * COLS, COLS)
                outs[k][4 + h, half * COLS : (half + 1) * COLS, :] = gt_ref[pl.ds(at, COLS), :]


def fetch(a_in, g_in, a_s, g_s, sems):
    copies = []
    for m in range(4):
        copies.append(pltpu.make_async_copy(a_in[m], a_s.at[m], sems.at[m]))
        copies.append(pltpu.make_async_copy(g_in[m], g_s.at[m], sems.at[4 + m]))
    for cp in copies:
        cp.start()
    for cp in copies:
        cp.wait()


def block_of(t, x, j, a_s, g_s):
    yh0, x0 = t // 4, t % 4
    k = (x + 4 - x0) % 4
    m = (j - yh0 - k + 8) % 4
    kg = (j + 4 - yh0) % 4
    mg = (x - x0 - kg + 8) % 4
    a = jnp.concatenate([a_s[m, k, r] for r in range(a_s.shape[2])], axis=1)
    gt = jnp.concatenate([g_s[mg, kg, h] for h in range(g_s.shape[2])], axis=0)
    return a, gt


def norm_kernel(pos, docs, *refs):
    a_in, g_in, out, a_s, g_s, acc, sems = refs[:4], refs[4:8], *refs[8:]
    x, j = pos[0], pos[2]
    fetch(a_in, g_in, a_s, g_s, sems)
    out[...] = jnp.zeros_like(out)
    lane = lax.broadcasted_iota(jnp.int32, (1, BLOCK), 1)

    def step(t, carry):
        d = docs[t]
        before = docs[jnp.maximum(t - 1, 0)]
        after = docs[jnp.minimum(t + 1, 15)]
        a, gt = block_of(t, x, j, a_s, g_s)
        new = jnp.dot(gt, a, preferred_element_type=jnp.float32)
        first = jnp.logical_or(t == 0, d != before)
        last = jnp.logical_or(t == 15, d != after)

        @pl.when(first)
        def _():
            acc[...] = new

        @pl.when(jnp.logical_not(first))
        def _():
            acc[...] = acc[...] + new

        @pl.when(last)
        def _():
            w = acc[...]
            total = jnp.sum(jnp.sum(w * w, axis=0, keepdims=True), axis=1, keepdims=True)
            out[...] = jnp.where(lane == d, total, out[...])

        return carry

    lax.fori_loop(0, 16, step, 0)


def grad_kernel(pos, docs, *refs):
    norms, a_in, g_in, out, clip_out, a_s, g_s, acc, sems = refs[0], refs[1:5], refs[5:9], *refs[9:]
    x, j = pos[0], pos[2]
    fetch(a_in, g_in, a_s, g_s, sems)
    norm_sq = jnp.sum(norms[...], axis=0)
    clip = CLIP / jnp.sqrt(jnp.maximum(norm_sq, CLIP * CLIP))
    clip_out[...] = clip
    lane = lax.broadcasted_iota(jnp.int32, (1, BLOCK), 1)

    def step(t, carry):
        a, gt = block_of(t, x, j, a_s, g_s)
        factor = jnp.sum(jnp.where(lane == docs[t], clip, 0.0), axis=1, keepdims=True)
        scaled = (gt.astype(jnp.float32) * factor).astype(jnp.bfloat16)
        new = jnp.dot(scaled, a, preferred_element_type=jnp.float32)

        @pl.when(t == 0)
        def _():
            acc[...] = new

        @pl.when(t != 0)
        def _():
            acc[...] = acc[...] + new

        return carry

    lax.fori_loop(0, 16, step, 0)
    for h in range(out.shape[0]):
        for y in range(4):
            out[h, y] = acc[h * COLS : (h + 1) * COLS, y * BLOCK : (y + 1) * BLOCK]


def body(sizes, activations, out_grads, segment_ids):
    a, g, ids = activations[0], out_grads[0], segment_ids
    heights = sizes["zh"]
    bf16 = jnp.bfloat16
    move = ("zl", "yl", "c", "yh", "x")
    x = lax.axis_index("x")
    yh = lax.axis_index("yh")
    j = lax.axis_index("zl") * 2 + lax.axis_index("c")
    pos = jnp.stack([x, yh, j]).astype(jnp.int32)
    smem = pl.BlockSpec(memory_space=pltpu.SMEM)
    vmem = pl.BlockSpec(memory_space=pltpu.VMEM)
    anywhere = pl.BlockSpec(memory_space=pl.ANY)

    payload = pl.pallas_call(
        prep_kernel,
        out_shape=[jax.ShapeDtypeStruct((4 + heights, BLOCK, BLOCK), bf16)] * 4,
        in_specs=[smem, vmem, vmem, vmem],
        out_specs=[vmem] * 4,
        scratch_shapes=[pltpu.VMEM((g.shape[1], BLOCK), bf16)],
        interpret=INTERPRET,
        name="prep",
    )(pos, ids, a, g)

    arrived = [
        lax.ppermute(payload[k], move, table(sizes, move, functools.partial(to_group, k))) for k in range(4)
    ]
    slab_doc = jnp.broadcast_to(jnp.max(ids, axis=1, keepdims=True), (1, BLOCK))
    slab_doc = lax.ppermute(slab_doc, move, table(sizes, move, functools.partial(to_group, 0)))
    group = ("zl", "c", "x")
    docs = lax.all_to_all(
        jnp.broadcast_to(slab_doc, (16, 1, BLOCK)), group, split_axis=0, concat_axis=0, tiled=True
    )[:, 0, 0]
    docs = jnp.where(docs < 0, DOCS, docs)

    own_a = jnp.stack([p[:4] for p in arrived])
    own_g = jnp.stack([p[4:] for p in arrived])
    a_parts = [own_a]
    g_parts = [own_g]
    for m in range(1, 4):
        g_parts.append(lax.ppermute(own_g, "x", [(s, (s + m) % 4) for s in range(4)]))
        a_parts.append(lax.ppermute(own_a, ("zl", "c"), [(s, (s + m) % 4) for s in range(4)]))

    stores = [
        pltpu.VMEM((4, 4, 4, BLOCK, BLOCK), bf16),
        pltpu.VMEM((4, 4, heights, BLOCK, BLOCK), bf16),
        pltpu.VMEM((heights * BLOCK, 4 * BLOCK), jnp.float32),
        pltpu.SemaphoreType.DMA((8,)),
    ]
    partial = pl.pallas_call(
        norm_kernel,
        out_shape=jax.ShapeDtypeStruct((1, BLOCK), jnp.float32),
        in_specs=[smem, smem] + [anywhere] * 8,
        out_specs=vmem,
        scratch_shapes=stores,
        interpret=INTERPRET,
        name="norms",
    )(pos, docs, *a_parts, *g_parts)
    norms = lax.all_to_all(
        jnp.broadcast_to(partial, (16, 1, BLOCK)), group, split_axis=0, concat_axis=0, tiled=True
    )
    pieces, clip = pl.pallas_call(
        grad_kernel,
        out_shape=[
            jax.ShapeDtypeStruct((heights * 2, 4, COLS, BLOCK), jnp.float32),
            jax.ShapeDtypeStruct((1, BLOCK), jnp.float32),
        ],
        in_specs=[smem, smem, vmem] + [anywhere] * 8,
        out_specs=[vmem, vmem],
        scratch_shapes=stores,
        interpret=INTERPRET,
        name="grads",
    )(pos, docs, norms, *a_parts, *g_parts)
    back = [(dst, src) for src, dst in table(sizes, move, functools.partial(to_group, 0))]
    clip = lax.ppermute(clip, move, back)
    pieces = pieces.reshape(heights * 8, COLS, BLOCK)
    summands = lax.all_to_all(pieces, ("zh", "yl", "yh"), split_axis=0, concat_axis=0, tiled=True)
    weight_grad = jnp.sum(summands, axis=0).T
    return weight_grad, clip[:, :DOCS]


def solution(mesh):
    heights = mesh.devices.size // 128
    dims = (heights, 2, 2, 2, 4, 4)
    fine = Mesh(mesh.devices.reshape(dims), AXES)
    dp, ctx = AXES[:4], AXES[4:]
    placed = (P(dp, ctx, None), P(dp, ctx, None), P(dp, ctx))
    return jax.shard_map(
        functools.partial(body, dict(zip(AXES, dims))),
        mesh=fine,
        in_specs=placed,
        out_specs=(P(ctx, dp), P(dp, None)),
        check_vma=False,
    )
```

```python
import functools

import jax
import jax.numpy as jnp
import numpy as np
from jax import lax
from jax.experimental import pallas as pl
from jax.experimental.pallas import tpu as pltpu
from jax.sharding import Mesh
from jax.sharding import PartitionSpec as P


INTERPRET = False
CLIP = 600.0
BLOCK = 128
COLS = 64
DOCS = 8
SLABS = 16
PART = 4 * BLOCK
TAIL = 8
PAD = 16

AXES = ("zh", "zl", "yl", "c", "yh", "x")
MOVE = ("yl", "c", "yh", "x")
GROUP = ("yl", "c", "x")
SUMMED = ("zh", "zl", "yh")


def table(sizes, axes, to):
    dims = [sizes[a] for a in axes]
    pairs = []
    for src in range(int(np.prod(dims))):
        at = dict(zip(axes, np.unravel_index(src, dims)))
        dst = to(**at)
        pairs.append((src, int(np.ravel_multi_index([int(dst[a]) for a in axes], dims))))
    return pairs


def to_group(k, yl, c, yh, x):
    j = (yh + k) % 4
    return dict(yl=j // 2, c=j % 2, yh=c * 2 + yl, x=(x + k) % 4)


def prep_kernel(pos, ids_ref, a_ref, g_ref, *rest):
    outs, gt_ref = rest[:4], rest[4]
    x, yh = pos[0], pos[1]
    chunks = g_ref.shape[1] // BLOCK
    ids = ids_ref[...]
    kept = ids >= 0
    doc = jnp.max(ids.astype(jnp.float32), axis=1, keepdims=True)
    doc = jnp.broadcast_to(doc, (PAD, BLOCK)).astype(jnp.bfloat16)
    for n in range(chunks):
        t = g_ref[:, n * BLOCK : (n + 1) * BLOCK].astype(jnp.float32).T
        gt_ref[n * BLOCK : (n + 1) * BLOCK, :] = jnp.where(kept, t, 0.0).astype(jnp.bfloat16)
    wide = chunks * BLOCK // 4
    for k in range(4):
        i = (x + k) % 4
        j = (yh + k) % 4
        for z in range(wide // COLS):
            at = pl.multiple_of((z * 4 + j) * COLS, COLS)
            outs[k][z * COLS : (z + 1) * COLS, :] = gt_ref[pl.ds(at, COLS), :]
        for r in range(4):
            at = pl.multiple_of((r * 4 + i) * BLOCK, BLOCK)
            outs[k][wide + r * BLOCK : wide + (r + 1) * BLOCK, :] = a_ref[:, pl.ds(at, BLOCK)]
        outs[k][wide + PART :, :] = doc


def fetch(pos, a_in, g_in, a_s, g_s, doc_s, sems):
    x, j = pos[0], pos[2]
    copies = []
    for m in range(4):
        for k in range(4):
            t = ((j ^ m) + 4 - k) % 4 * 4 + (x + 4 - k) % 4
            at = pl.multiple_of(t * BLOCK, BLOCK)
            for r in range(4):
                copies.append(
                    pltpu.make_async_copy(
                        a_in[m].at[k, r * BLOCK : (r + 1) * BLOCK],
                        a_s.at[pl.ds(at, BLOCK), r * BLOCK : (r + 1) * BLOCK],
                        sems.at[len(copies)],
                    )
                )
            copies.append(pltpu.make_async_copy(a_in[m].at[k, PART:], doc_s.at[t], sems.at[len(copies)]))
            t = (j + 4 - k) % 4 * 4 + (x + 8 - m - k) % 4
            at = pl.multiple_of(t * BLOCK, BLOCK)
            copies.append(pltpu.make_async_copy(g_in[m].at[k], g_s.at[:, pl.ds(at, BLOCK)], sems.at[len(copies)]))
    for cp in copies:
        cp.start()
    for cp in copies:
        cp.wait()


COPIES = 16 * 6


def norm_kernel(pos, *refs):
    a_in, g_in, out, a_s, g_s, doc_s, acc, starts, sems = refs[:4], refs[4:8], *refs[8:]
    fetch(pos, a_in, g_in, a_s, g_s, doc_s, sems)
    a_s[SLABS * BLOCK :, :] = jnp.zeros((BLOCK, a_s.shape[1]), a_s.dtype)
    out[...] = jnp.zeros_like(out)
    doc = jnp.int32(-1)
    for t in range(SLABS):
        here = jnp.maximum(doc, jnp.max(doc_s[t].astype(jnp.float32)).astype(jnp.int32))
        new = here != doc

        @pl.when(new)
        def _(here=here, t=t):
            starts[here] = t

        doc = here
    starts[DOCS] = SLABS
    lane = lax.broadcasted_iota(jnp.int32, (1, BLOCK), 1)
    second = lax.broadcasted_iota(jnp.int32, (1, 2 * BLOCK), 1) >= BLOCK

    def product(first, end):
        at = pl.multiple_of(first * BLOCK, BLOCK)
        g = g_s[:, pl.ds(at, 2 * BLOCK)]
        g = jnp.where(jnp.logical_and(second, first + 1 >= end), jnp.zeros_like(g), g)
        return jnp.dot(g, a_s[pl.ds(at, 2 * BLOCK), :], preferred_element_type=jnp.float32)

    def squared(w, d):
        total = jnp.sum(jnp.sum(w * w, axis=0, keepdims=True), axis=1, keepdims=True)
        out[...] = jnp.where(lane == d, total, out[...])

    def document(d, carry):
        first, end = starts[d], starts[d + 1]

        @pl.when(end - first <= 2)
        def _():
            squared(product(first, end), d)

        @pl.when(end - first > 2)
        def _():
            acc[...] = product(first, end)

            def more(n, c):
                acc[...] = acc[...] + product(first + 2 * n, end)
                return c

            lax.fori_loop(1, (end - first + 1) // 2, more, 0)
            squared(acc[...], d)

        return carry

    lax.fori_loop(0, DOCS, document, 0)


def grad_kernel(pos, *refs):
    norms, own, a_in, g_in = refs[0], refs[1], refs[2:6], refs[6:10]
    out, clip_out, a_s, g_s, doc_s, acc, sems = refs[10:]
    fetch(pos, a_in, g_in, a_s, g_s, doc_s, sems)
    norm_sq = jnp.sum(norms[...], axis=0)
    clip = CLIP / jnp.sqrt(jnp.maximum(norm_sq, CLIP * CLIP))
    clip_out[...] = clip
    bound = jnp.sum(jnp.minimum(jnp.sqrt(own[...]), CLIP), axis=1, keepdims=True)
    shift = jnp.ceil(jnp.log2(jnp.maximum(bound, 1e-18))) - 14.0
    lane = lax.broadcasted_iota(jnp.int32, (1, BLOCK), 1).astype(jnp.float32)
    for t in range(SLABS):
        here = doc_s[t, 0:1, :].astype(jnp.float32) == lane
        factor = jnp.sum(jnp.where(here, clip, 0.0), axis=1, keepdims=True)
        g = g_s[:, t * BLOCK : (t + 1) * BLOCK].astype(jnp.float32)
        g_s[:, t * BLOCK : (t + 1) * BLOCK] = (g * factor).astype(jnp.bfloat16)
    tokens = SLABS * BLOCK
    acc[...] = jnp.dot(g_s[:, :tokens], a_s[:tokens, :], preferred_element_type=jnp.float32)
    scale = jnp.exp2(-shift)
    tail = jnp.broadcast_to(shift, (TAIL, BLOCK))
    for z in range(out.shape[0]):
        for y in range(4):
            piece = acc[z * COLS : (z + 1) * COLS, y * BLOCK : (y + 1) * BLOCK]
            out[z, y, :COLS] = piece * scale
            out[z, y, COLS:] = tail


def body(sizes, activations, out_grads, segment_ids):
    a, g, ids = activations[0], out_grads[0], segment_ids
    levels = sizes["zh"] * sizes["zl"]
    wide = levels * COLS
    bf16, f32 = jnp.bfloat16, jnp.float32
    x = lax.axis_index("x")
    yh = lax.axis_index("yh")
    j = lax.axis_index("yl") * 2 + lax.axis_index("c")
    pos = jnp.stack([x, yh, j]).astype(jnp.int32)
    smem = pl.BlockSpec(memory_space=pltpu.SMEM)
    vmem = pl.BlockSpec(memory_space=pltpu.VMEM)
    anywhere = pl.BlockSpec(memory_space=pl.ANY)

    payload = pl.pallas_call(
        prep_kernel,
        out_shape=[jax.ShapeDtypeStruct((wide + PART + PAD, BLOCK), bf16)] * 4,
        in_specs=[smem, vmem, vmem, vmem],
        out_specs=[vmem] * 4,
        scratch_shapes=[pltpu.VMEM((g.shape[1], BLOCK), bf16)],
        interpret=INTERPRET,
        name="prep",
    )(pos, ids, a, g)

    arrived = [
        lax.ppermute(payload[k], MOVE, table(sizes, MOVE, functools.partial(to_group, k))) for k in range(4)
    ]
    own_g = jnp.stack([p[:wide] for p in arrived])
    own_a = jnp.stack([p[wide:] for p in arrived])
    flip = [(0, 1), (1, 0)]
    partner = lax.ppermute(own_a, "yl", flip)
    g_parts = [own_g] + [lax.ppermute(own_g, "x", [(s, (s + m) % 4) for s in range(4)]) for m in (1, 2, 3)]
    a_parts = [own_a, lax.ppermute(own_a, "c", flip), partner, lax.ppermute(partner, "c", flip)]

    stores = [
        pltpu.VMEM(((SLABS + 1) * BLOCK, PART), bf16),
        pltpu.VMEM((wide, (SLABS + 1) * BLOCK), bf16),
        pltpu.VMEM((SLABS, PAD, BLOCK), bf16),
        pltpu.VMEM((wide, PART), f32),
    ]
    sems = [pltpu.SemaphoreType.DMA((COPIES,))]
    row = jax.ShapeDtypeStruct((1, BLOCK), f32)
    partial = pl.pallas_call(
        norm_kernel,
        out_shape=row,
        in_specs=[smem] + [anywhere] * 8,
        out_specs=vmem,
        scratch_shapes=stores + [pltpu.SMEM((DOCS + 1,), jnp.int32)] + sems,
        interpret=INTERPRET,
        name="norms",
    )(pos, *a_parts, *g_parts)
    norms = lax.all_to_all(
        jnp.broadcast_to(partial, (16, 1, BLOCK)), GROUP, split_axis=0, concat_axis=0, tiled=True
    )
    pieces, clip = pl.pallas_call(
        grad_kernel,
        out_shape=[jax.ShapeDtypeStruct((levels, 4, COLS + TAIL, BLOCK), f32), row],
        in_specs=[smem, vmem, vmem] + [anywhere] * 8,
        out_specs=[vmem] * 2,
        scratch_shapes=stores + sems,
        interpret=INTERPRET,
        name="grads",
    )(pos, norms, partial, *a_parts, *g_parts)
    pieces = pieces.astype(jnp.float16).reshape(levels * 4, COLS + TAIL, BLOCK)
    summands = lax.all_to_all(pieces, SUMMED, split_axis=0, concat_axis=0, tiled=True).astype(f32)
    weight_grad = jnp.sum(summands[:, :COLS] * jnp.exp2(summands[:, COLS : COLS + 1]), axis=0).T
    home = [(dst, src) for src, dst in table(sizes, MOVE, functools.partial(to_group, 0))]
    clip = lax.ppermute(clip, MOVE, home)
    return weight_grad, clip[:, :DOCS]


def solution(mesh):
    heights = mesh.devices.size // 128
    dims = (heights, 2, 2, 2, 4, 4)
    fine = Mesh(mesh.devices.reshape(dims), AXES)
    dp, ctx = AXES[:4], AXES[4:]
    placed = (P(dp, ctx, None), P(dp, ctx, None), P(dp, ctx))
    return jax.shard_map(
        functools.partial(body, dict(zip(AXES, dims))),
        mesh=fine,
        in_specs=placed,
        out_specs=(P(ctx, dp), P(dp, None)),
        check_vma=False,
    )
```

```python
import functools

import jax
import jax.numpy as jnp
import numpy as np
from jax import lax
from jax.experimental import pallas as pl
from jax.experimental.pallas import tpu as pltpu
from jax.sharding import Mesh
from jax.sharding import PartitionSpec as P


INTERPRET = False
CLIP = 600.0
BLOCK = 128
COLS = 64
DOCS = 8
SLABS = 16
PART = 4 * BLOCK
TAIL = 8
PAD = 16

AXES = ("zh", "zl", "yl", "c", "yh", "x")
MOVE = ("yl", "c", "yh", "x")
GROUP = ("yl", "c", "x")
SUMMED = ("zh", "zl", "yh")


def table(sizes, axes, to):
    dims = [sizes[a] for a in axes]
    pairs = []
    for src in range(int(np.prod(dims))):
        at = dict(zip(axes, np.unravel_index(src, dims)))
        dst = to(**at)
        pairs.append((src, int(np.ravel_multi_index([int(dst[a]) for a in axes], dims))))
    return pairs


def to_group(k, yl, c, yh, x):
    j = (yh + k) % 4
    return dict(yl=j // 2, c=j % 2, yh=c * 2 + yl, x=(x + k) % 4)


def prep_kernel(pos, ids_ref, a_ref, g_ref, *rest):
    outs, gt_ref = rest[:4], rest[4]
    x, yh = pos[0], pos[1]
    chunks = g_ref.shape[1] // BLOCK
    ids = ids_ref[...]
    kept = ids >= 0
    doc = jnp.max(ids.astype(jnp.float32), axis=1, keepdims=True)
    doc = jnp.broadcast_to(doc, (PAD, BLOCK)).astype(jnp.bfloat16)
    for n in range(chunks):
        t = g_ref[:, n * BLOCK : (n + 1) * BLOCK].astype(jnp.float32).T
        gt_ref[n * BLOCK : (n + 1) * BLOCK, :] = jnp.where(kept, t, 0.0).astype(jnp.bfloat16)
    wide = chunks * BLOCK // 4
    for k in range(4):
        i = (x + k) % 4
        j = (yh + k) % 4
        for z in range(wide // COLS):
            at = pl.multiple_of((z * 4 + j) * COLS, COLS)
            outs[k][z * COLS : (z + 1) * COLS, :] = gt_ref[pl.ds(at, COLS), :]
        for r in range(4):
            at = pl.multiple_of((r * 4 + i) * BLOCK, BLOCK)
            outs[k][wide + r * BLOCK : wide + (r + 1) * BLOCK, :] = a_ref[:, pl.ds(at, BLOCK)]
        outs[k][wide + PART :, :] = doc


def fetch(pos, parts, a_s, g_s, doc_s, sems):
    x, j = pos[0], pos[2]
    copies = []

    def copy(src, dst):
        copies.append(pltpu.make_async_copy(src, dst, sems.at[len(copies)]))

    for k in range(4):
        own, partner, other, spread = parts[k // 2 :: 2]
        n = k % 2
        for m, src in enumerate((own, other.at[0], partner, other.at[1])):
            t = ((j ^ m) + 4 - k) % 4 * 4 + (x + 4 - k) % 4
            at = pl.multiple_of(t * BLOCK, BLOCK)
            for r in range(4):
                rows = slice(r * BLOCK, (r + 1) * BLOCK)
                copy(src.at[n, rows], a_s.at[pl.ds(at, BLOCK), rows])
            copy(src.at[n, PART:], doc_s.at[t])
        for sender in range(4):
            t = (j + 4 - k) % 4 * 4 + (sender + 4 - k) % 4
            at = pl.multiple_of(t * BLOCK, BLOCK)
            copy(spread.at[sender, n], g_s.at[:, pl.ds(at, BLOCK)])
    for cp in copies:
        cp.start()
    for cp in copies:
        cp.wait()


COPIES = 16 * 6


def norm_kernel(pos, *refs):
    parts, out, a_s, g_s, doc_s, acc, starts, sems = refs[:8], *refs[8:]
    fetch(pos, parts, a_s, g_s, doc_s, sems)
    a_s[SLABS * BLOCK :, :] = jnp.zeros((BLOCK, a_s.shape[1]), a_s.dtype)
    out[...] = jnp.zeros_like(out)
    doc = jnp.int32(-1)
    for t in range(SLABS):
        here = jnp.maximum(doc, jnp.max(doc_s[t].astype(jnp.float32)).astype(jnp.int32))
        new = here != doc

        @pl.when(new)
        def _(here=here, t=t):
            starts[here] = t

        doc = here
    starts[DOCS] = SLABS
    lane = lax.broadcasted_iota(jnp.int32, (1, BLOCK), 1)
    second = lax.broadcasted_iota(jnp.int32, (1, 2 * BLOCK), 1) >= BLOCK

    def product(first, end):
        at = pl.multiple_of(first * BLOCK, BLOCK)
        g = g_s[:, pl.ds(at, 2 * BLOCK)]
        g = jnp.where(jnp.logical_and(second, first + 1 >= end), jnp.zeros_like(g), g)
        return jnp.dot(g, a_s[pl.ds(at, 2 * BLOCK), :], preferred_element_type=jnp.float32)

    def squared(w, d):
        total = jnp.sum(jnp.sum(w * w, axis=0, keepdims=True), axis=1, keepdims=True)
        out[...] = jnp.where(lane == d, total, out[...])

    def document(d, carry):
        first, end = starts[d], starts[d + 1]

        @pl.when(end - first <= 2)
        def _():
            squared(product(first, end), d)

        @pl.when(end - first > 2)
        def _():
            acc[...] = product(first, end)

            def more(n, c):
                acc[...] = acc[...] + product(first + 2 * n, end)
                return c

            lax.fori_loop(1, (end - first + 1) // 2, more, 0)
            squared(acc[...], d)

        return carry

    lax.fori_loop(0, DOCS, document, 0)


def grad_kernel(pos, *refs):
    norms, own, parts = refs[0], refs[1], refs[2:10]
    out, clip_out, a_s, g_s, doc_s, acc, sems = refs[10:]
    fetch(pos, parts, a_s, g_s, doc_s, sems)
    norm_sq = jnp.sum(norms[...], axis=0)
    clip = CLIP / jnp.sqrt(jnp.maximum(norm_sq, CLIP * CLIP))
    clip_out[...] = clip
    bound = jnp.sum(jnp.minimum(jnp.sqrt(own[...]), CLIP), axis=1, keepdims=True)
    shift = jnp.ceil(jnp.log2(jnp.maximum(bound, 1e-18))) - 14.0
    lane = lax.broadcasted_iota(jnp.int32, (1, BLOCK), 1).astype(jnp.float32)
    for t in range(SLABS):
        here = doc_s[t, 0:1, :].astype(jnp.float32) == lane
        factor = jnp.sum(jnp.where(here, clip, 0.0), axis=1, keepdims=True)
        g = g_s[:, t * BLOCK : (t + 1) * BLOCK].astype(jnp.float32)
        g_s[:, t * BLOCK : (t + 1) * BLOCK] = (g * factor).astype(jnp.bfloat16)
    tokens = SLABS * BLOCK
    acc[...] = jnp.dot(g_s[:, :tokens], a_s[:tokens, :], preferred_element_type=jnp.float32)
    scale = jnp.exp2(-shift)
    tail = jnp.broadcast_to(shift, (TAIL, BLOCK))
    for z in range(out.shape[0]):
        for y in range(4):
            piece = acc[z * COLS : (z + 1) * COLS, y * BLOCK : (y + 1) * BLOCK]
            out[z, y, :COLS] = piece * scale
            out[z, y, COLS:] = tail


def body(sizes, activations, out_grads, segment_ids):
    a, g, ids = activations[0], out_grads[0], segment_ids
    levels = sizes["zh"] * sizes["zl"]
    wide = levels * COLS
    bf16, f32 = jnp.bfloat16, jnp.float32
    x = lax.axis_index("x")
    yh = lax.axis_index("yh")
    j = lax.axis_index("yl") * 2 + lax.axis_index("c")
    pos = jnp.stack([x, yh, j]).astype(jnp.int32)
    smem = pl.BlockSpec(memory_space=pltpu.SMEM)
    vmem = pl.BlockSpec(memory_space=pltpu.VMEM)
    anywhere = pl.BlockSpec(memory_space=pl.ANY)

    payload = pl.pallas_call(
        prep_kernel,
        out_shape=[jax.ShapeDtypeStruct((wide + PART + PAD, BLOCK), bf16)] * 4,
        in_specs=[smem, vmem, vmem, vmem],
        out_specs=[vmem] * 4,
        scratch_shapes=[pltpu.VMEM((g.shape[1], BLOCK), bf16)],
        interpret=INTERPRET,
        name="prep",
    )(pos, ids, a, g)

    arrived = [
        lax.ppermute(payload[k], MOVE, table(sizes, MOVE, functools.partial(to_group, k))) for k in range(4)
    ]
    flip = [(0, 1), (1, 0)]
    own_a, partner, other, spread = [], [], [], []
    for n in range(2):
        two = arrived[2 * n : 2 * n + 2]
        own_g = jnp.stack([p[:wide] for p in two])
        spread.append(
            lax.all_to_all(
                jnp.broadcast_to(own_g, (4, *own_g.shape)), "x", split_axis=0, concat_axis=0, tiled=True
            )
        )
        own_a.append(jnp.stack([p[wide:] for p in two]))
        partner.append(lax.ppermute(own_a[n], "yl", flip))
        other.append(lax.ppermute(jnp.stack([own_a[n], partner[n]]), "c", flip))
    parts = own_a + partner + other + spread

    stores = [
        pltpu.VMEM(((SLABS + 1) * BLOCK, PART), bf16),
        pltpu.VMEM((wide, (SLABS + 1) * BLOCK), bf16),
        pltpu.VMEM((SLABS, PAD, BLOCK), bf16),
        pltpu.VMEM((wide, PART), f32),
    ]
    sems = [pltpu.SemaphoreType.DMA((COPIES,))]
    row = jax.ShapeDtypeStruct((1, BLOCK), f32)
    partial = pl.pallas_call(
        norm_kernel,
        out_shape=row,
        in_specs=[smem] + [anywhere] * 8,
        out_specs=vmem,
        scratch_shapes=stores + [pltpu.SMEM((DOCS + 1,), jnp.int32)] + sems,
        interpret=INTERPRET,
        name="norms",
    )(pos, *parts)
    norms = lax.all_to_all(
        jnp.broadcast_to(partial, (16, 1, BLOCK)), GROUP, split_axis=0, concat_axis=0, tiled=True
    )
    pieces, clip = pl.pallas_call(
        grad_kernel,
        out_shape=[jax.ShapeDtypeStruct((levels, 4, COLS + TAIL, BLOCK), f32), row],
        in_specs=[smem, vmem, vmem] + [anywhere] * 8,
        out_specs=[vmem] * 2,
        scratch_shapes=stores + sems,
        interpret=INTERPRET,
        name="grads",
    )(pos, norms, partial, *parts)
    pieces = pieces.astype(jnp.float16).reshape(levels * 4, COLS + TAIL, BLOCK)
    summands = lax.all_to_all(pieces, SUMMED, split_axis=0, concat_axis=0, tiled=True).astype(f32)
    weight_grad = jnp.sum(summands[:, :COLS] * jnp.exp2(summands[:, COLS : COLS + 1]), axis=0).T
    home = [(dst, src) for src, dst in table(sizes, MOVE, functools.partial(to_group, 0))]
    clip = lax.ppermute(clip, MOVE, home)
    return weight_grad, clip[:, :DOCS]


def solution(mesh):
    heights = mesh.devices.size // 128
    dims = (heights, 2, 2, 2, 4, 4)
    fine = Mesh(mesh.devices.reshape(dims), AXES)
    dp, ctx = AXES[:4], AXES[4:]
    placed = (P(dp, ctx, None), P(dp, ctx, None), P(dp, ctx))
    return jax.shard_map(
        functools.partial(body, dict(zip(AXES, dims))),
        mesh=fine,
        in_specs=placed,
        out_specs=(P(ctx, dp), P(dp, None)),
        check_vma=False,
    )
```

```python
import functools

import jax
import jax.numpy as jnp
import numpy as np
from jax import lax
from jax.experimental import pallas as pl
from jax.experimental.pallas import tpu as pltpu
from jax.sharding import Mesh
from jax.sharding import PartitionSpec as P


INTERPRET = False
CLIP = 600.0
BLOCK = 128
COLS = 64
DOCS = 8
SLABS = 16
PART = 4 * BLOCK
TAIL = 8
PAD = 16

AXES = ("zh", "zl", "yl", "c", "yh", "x")
MOVE = ("yl", "c", "yh", "x")
GROUP = ("yl", "c", "x")
SUMMED = ("zh", "zl", "yh")


def table(sizes, axes, to):
    dims = [sizes[a] for a in axes]
    pairs = []
    for src in range(int(np.prod(dims))):
        at = dict(zip(axes, np.unravel_index(src, dims)))
        dst = to(**at)
        pairs.append((src, int(np.ravel_multi_index([int(dst[a]) for a in axes], dims))))
    return pairs


def to_group(k, yl, c, yh, x):
    j = (yh + k) % 4
    return dict(yl=j // 2, c=j % 2, yh=c * 2 + yl, x=(x + k) % 4)


def prep_kernel(pos, ids_ref, a_ref, g_ref, *rest):
    outs, gt_ref = rest[:4], rest[4]
    x, yh = pos[0], pos[1]
    chunks = g_ref.shape[1] // BLOCK
    ids = ids_ref[...]
    kept = ids >= 0
    doc = jnp.max(ids.astype(jnp.float32), axis=1, keepdims=True)
    doc = jnp.broadcast_to(doc, (PAD, BLOCK)).astype(jnp.bfloat16)
    for n in range(chunks):
        t = g_ref[:, n * BLOCK : (n + 1) * BLOCK].astype(jnp.float32).T
        gt_ref[n * BLOCK : (n + 1) * BLOCK, :] = jnp.where(kept, t, 0.0).astype(jnp.bfloat16)
    wide = chunks * BLOCK // 4
    for k in range(4):
        i = (x + k) % 4
        j = (yh + k) % 4
        for z in range(wide // COLS):
            at = pl.multiple_of((z * 4 + j) * COLS, COLS)
            outs[k][z * COLS : (z + 1) * COLS, :] = gt_ref[pl.ds(at, COLS), :]
        for r in range(4):
            at = pl.multiple_of((r * 4 + i) * BLOCK, BLOCK)
            outs[k][wide + r * BLOCK : wide + (r + 1) * BLOCK, :] = a_ref[:, pl.ds(at, BLOCK)]
        outs[k][wide + PART :, :] = doc


def fetch(pos, parts, a_s, g_s, doc_s, sems):
    x, j = pos[0], pos[2]
    copies = []

    def copy(src, dst):
        copies.append(pltpu.make_async_copy(src, dst, sems.at[len(copies)]))

    for k in range(4):
        for m in range(4):
            t = ((j ^ m) + 4 - k) % 4 * 4 + (x + 4 - k) % 4
            at = pl.multiple_of(t * BLOCK, BLOCK)
            for r in range(4):
                rows = slice(r * BLOCK, (r + 1) * BLOCK)
                copy(parts[m].at[k, rows], a_s.at[pl.ds(at, BLOCK), rows])
            copy(parts[m].at[k, PART:], doc_s.at[t])
        for m in range(4):
            if k < 2:
                src, sender = parts[4 + m].at[k], (x + 4 - m) % 4
            else:
                src, sender = parts[8].at[m, k - 2], m
            t = (j + 4 - k) % 4 * 4 + (sender + 4 - k) % 4
            at = pl.multiple_of(t * BLOCK, BLOCK)
            copy(src, g_s.at[:, pl.ds(at, BLOCK)])
    for cp in copies:
        cp.start()
    for cp in copies:
        cp.wait()


COPIES = 16 * 6


def norm_kernel(pos, *refs):
    parts, out, a_s, g_s, doc_s, acc, starts, sems = refs[:9], *refs[9:]
    fetch(pos, parts, a_s, g_s, doc_s, sems)
    a_s[SLABS * BLOCK :, :] = jnp.zeros((BLOCK, a_s.shape[1]), a_s.dtype)
    out[...] = jnp.zeros_like(out)
    doc = jnp.int32(-1)
    for t in range(SLABS):
        here = jnp.maximum(doc, jnp.max(doc_s[t].astype(jnp.float32)).astype(jnp.int32))
        new = here != doc

        @pl.when(new)
        def _(here=here, t=t):
            starts[here] = t

        doc = here
    starts[DOCS] = SLABS
    lane = lax.broadcasted_iota(jnp.int32, (1, BLOCK), 1)
    second = lax.broadcasted_iota(jnp.int32, (1, 2 * BLOCK), 1) >= BLOCK

    def product(first, end):
        at = pl.multiple_of(first * BLOCK, BLOCK)
        g = g_s[:, pl.ds(at, 2 * BLOCK)]
        g = jnp.where(jnp.logical_and(second, first + 1 >= end), jnp.zeros_like(g), g)
        return jnp.dot(g, a_s[pl.ds(at, 2 * BLOCK), :], preferred_element_type=jnp.float32)

    def squared(w, d):
        total = jnp.sum(jnp.sum(w * w, axis=0, keepdims=True), axis=1, keepdims=True)
        out[...] = jnp.where(lane == d, total, out[...])

    def document(d, carry):
        first, end = starts[d], starts[d + 1]

        @pl.when(end - first <= 2)
        def _():
            squared(product(first, end), d)

        @pl.when(end - first > 2)
        def _():
            acc[...] = product(first, end)

            def more(n, c):
                acc[...] = acc[...] + product(first + 2 * n, end)
                return c

            lax.fori_loop(1, (end - first + 1) // 2, more, 0)
            squared(acc[...], d)

        return carry

    lax.fori_loop(0, DOCS, document, 0)


def grad_kernel(pos, *refs):
    norms, own, parts = refs[0], refs[1], refs[2:11]
    out, clip_out, a_s, g_s, doc_s, acc, sems = refs[11:]
    fetch(pos, parts, a_s, g_s, doc_s, sems)
    norm_sq = jnp.sum(norms[...], axis=0)
    clip = CLIP / jnp.sqrt(jnp.maximum(norm_sq, CLIP * CLIP))
    clip_out[...] = clip
    bound = jnp.sum(jnp.minimum(jnp.sqrt(own[...]), CLIP), axis=1, keepdims=True)
    shift = jnp.ceil(jnp.log2(jnp.maximum(bound, 1e-18))) - 14.0
    lane = lax.broadcasted_iota(jnp.int32, (1, BLOCK), 1).astype(jnp.float32)
    for t in range(SLABS):
        here = doc_s[t, 0:1, :].astype(jnp.float32) == lane
        factor = jnp.sum(jnp.where(here, clip, 0.0), axis=1, keepdims=True)
        g = g_s[:, t * BLOCK : (t + 1) * BLOCK].astype(jnp.float32)
        g_s[:, t * BLOCK : (t + 1) * BLOCK] = (g * factor).astype(jnp.bfloat16)
    tokens = SLABS * BLOCK
    acc[...] = jnp.dot(g_s[:, :tokens], a_s[:tokens, :], preferred_element_type=jnp.float32)
    scale = jnp.exp2(-shift)
    tail = jnp.broadcast_to(shift, (TAIL, BLOCK))
    for z in range(out.shape[0]):
        for y in range(4):
            piece = acc[z * COLS : (z + 1) * COLS, y * BLOCK : (y + 1) * BLOCK]
            out[z, y, :COLS] = piece * scale
            out[z, y, COLS:] = tail


def body(sizes, activations, out_grads, segment_ids):
    a, g, ids = activations[0], out_grads[0], segment_ids
    levels = sizes["zh"] * sizes["zl"]
    wide = levels * COLS
    bf16, f32 = jnp.bfloat16, jnp.float32
    x = lax.axis_index("x")
    yh = lax.axis_index("yh")
    j = lax.axis_index("yl") * 2 + lax.axis_index("c")
    pos = jnp.stack([x, yh, j]).astype(jnp.int32)
    smem = pl.BlockSpec(memory_space=pltpu.SMEM)
    vmem = pl.BlockSpec(memory_space=pltpu.VMEM)
    anywhere = pl.BlockSpec(memory_space=pl.ANY)

    payload = pl.pallas_call(
        prep_kernel,
        out_shape=[jax.ShapeDtypeStruct((wide + PART + PAD, BLOCK), bf16)] * 4,
        in_specs=[smem, vmem, vmem, vmem],
        out_specs=[vmem] * 4,
        scratch_shapes=[pltpu.VMEM((g.shape[1], BLOCK), bf16)],
        interpret=INTERPRET,
        name="prep",
    )(pos, ids, a, g)

    arrived = [
        lax.ppermute(payload[k], MOVE, table(sizes, MOVE, functools.partial(to_group, k))) for k in range(4)
    ]
    flip = [(0, 1), (1, 0)]
    last_g = jnp.stack([p[:wide] for p in arrived[2:]])
    last_g = lax.all_to_all(
        jnp.broadcast_to(last_g, (4, *last_g.shape)), "x", split_axis=0, concat_axis=0, tiled=True
    )
    own_a = jnp.stack([p[wide:] for p in arrived])
    own_g = jnp.stack([p[:wide] for p in arrived[:2]])
    partner = lax.ppermute(own_a, "yl", flip)
    own_other = lax.ppermute(own_a, "c", flip)
    g_parts = [own_g]
    for m in (1, 2, 3):
        g_parts.append(lax.ppermute(own_g, "x", [(s, (s + m) % 4) for s in range(4)]))
    partner_other = lax.ppermute(partner, "c", flip)
    a_parts = [own_a, own_other, partner, partner_other]
    parts = a_parts + g_parts + [last_g]

    stores = [
        pltpu.VMEM(((SLABS + 1) * BLOCK, PART), bf16),
        pltpu.VMEM((wide, (SLABS + 1) * BLOCK), bf16),
        pltpu.VMEM((SLABS, PAD, BLOCK), bf16),
        pltpu.VMEM((wide, PART), f32),
    ]
    sems = [pltpu.SemaphoreType.DMA((COPIES,))]
    row = jax.ShapeDtypeStruct((1, BLOCK), f32)
    partial = pl.pallas_call(
        norm_kernel,
        out_shape=row,
        in_specs=[smem] + [anywhere] * 9,
        out_specs=vmem,
        scratch_shapes=stores + [pltpu.SMEM((DOCS + 1,), jnp.int32)] + sems,
        interpret=INTERPRET,
        name="norms",
    )(pos, *parts)
    norms = lax.all_to_all(
        jnp.broadcast_to(partial, (16, 1, BLOCK)), GROUP, split_axis=0, concat_axis=0, tiled=True
    )
    pieces, clip = pl.pallas_call(
        grad_kernel,
        out_shape=[jax.ShapeDtypeStruct((levels, 4, COLS + TAIL, BLOCK), f32), row],
        in_specs=[smem, vmem, vmem] + [anywhere] * 9,
        out_specs=[vmem] * 2,
        scratch_shapes=stores + sems,
        interpret=INTERPRET,
        name="grads",
    )(pos, norms, partial, *parts)
    pieces = pieces.astype(jnp.float16).reshape(levels * 4, COLS + TAIL, BLOCK)
    summands = lax.all_to_all(pieces, SUMMED, split_axis=0, concat_axis=0, tiled=True).astype(f32)
    weight_grad = jnp.sum(summands[:, :COLS] * jnp.exp2(summands[:, COLS : COLS + 1]), axis=0).T
    home = [(dst, src) for src, dst in table(sizes, MOVE, functools.partial(to_group, 0))]
    clip = lax.ppermute(clip, MOVE, home)
    return weight_grad, clip[:, :DOCS]


def solution(mesh):
    heights = mesh.devices.size // 128
    dims = (heights, 2, 2, 2, 4, 4)
    fine = Mesh(mesh.devices.reshape(dims), AXES)
    dp, ctx = AXES[:4], AXES[4:]
    placed = (P(dp, ctx, None), P(dp, ctx, None), P(dp, ctx))
    return jax.shard_map(
        functools.partial(body, dict(zip(AXES, dims))),
        mesh=fine,
        in_specs=placed,
        out_specs=(P(ctx, dp), P(dp, None)),
        check_vma=False,
    )
```

```python
import functools

import jax
import jax.numpy as jnp
import numpy as np
from jax import lax
from jax.experimental import pallas as pl
from jax.experimental.pallas import tpu as pltpu
from jax.sharding import Mesh
from jax.sharding import PartitionSpec as P


INTERPRET = False
CLIP = 600.0
BLOCK = 128
COLS = 64
DOCS = 8
SLABS = 16
PART = 4 * BLOCK
TAIL = 8
PAD = 16

ORDER = (1, 3, 0, 2)
AXES = ("zh", "zl", "yl", "c", "yh", "x")
MOVE = ("yl", "c", "yh", "x")
GROUP = ("yl", "c", "x")
SUMMED = ("zh", "zl", "yh")


def table(sizes, axes, to):
    dims = [sizes[a] for a in axes]
    pairs = []
    for src in range(int(np.prod(dims))):
        at = dict(zip(axes, np.unravel_index(src, dims)))
        dst = to(**at)
        pairs.append((src, int(np.ravel_multi_index([int(dst[a]) for a in axes], dims))))
    return pairs


def to_group(k, yl, c, yh, x):
    j = (yh + k) % 4
    return dict(yl=j // 2, c=j % 2, yh=c * 2 + yl, x=(x + k) % 4)


def prep_kernel(ids_ref, a_ref, g_ref, *rest):
    outs, gt_ref = rest[:4], rest[4]
    x, yh = lax.axis_index("x"), lax.axis_index("yh")
    chunks = g_ref.shape[1] // BLOCK
    ids = ids_ref[...]
    kept = ids >= 0
    doc = jnp.max(ids.astype(jnp.float32), axis=1, keepdims=True)
    doc = jnp.broadcast_to(doc, (PAD, BLOCK)).astype(jnp.bfloat16)
    for n in range(chunks):
        t = g_ref[:, n * BLOCK : (n + 1) * BLOCK].astype(jnp.float32).T
        gt_ref[n * BLOCK : (n + 1) * BLOCK, :] = jnp.where(kept, t, 0.0).astype(jnp.bfloat16)
    wide = chunks * BLOCK // 4
    for n, k in enumerate(ORDER):
        i = (x + k) % 4
        j = (yh + k) % 4
        for z in range(wide // COLS):
            at = pl.multiple_of((z * 4 + j) * COLS, COLS)
            outs[n][z * COLS : (z + 1) * COLS, :] = gt_ref[pl.ds(at, COLS), :]
        for r in range(4):
            at = pl.multiple_of((r * 4 + i) * BLOCK, BLOCK)
            outs[n][wide + r * BLOCK : wide + (r + 1) * BLOCK, :] = a_ref[:, pl.ds(at, BLOCK)]
        outs[n][wide + PART :, :] = doc


def fetch(parts, a_s, g_s, doc_s, sems):
    x, j = lax.axis_index("x"), lax.axis_index("yl") * 2 + lax.axis_index("c")
    copies = []

    def copy(src, dst):
        copies.append(pltpu.make_async_copy(src, dst, sems.at[len(copies)]))

    def slab(j, k, x):
        return (j + 4 - k) % 4 * 4 + (x + 4 - k) % 4

    for n, k in enumerate(ORDER):
        for m in range(4):
            copy(parts[m].at[n, PART:], doc_s.at[slab(j ^ m, k, x)])
    for n, k in enumerate(ORDER):
        for m in range(4):
            if n < 2:
                src, sender = parts[4 + m].at[n], (x + 4 - m) % 4
            else:
                src, sender = parts[8].at[m, n - 2], m
            at = pl.multiple_of(slab(j, k, sender) * BLOCK, BLOCK)
            copy(src, g_s.at[:, pl.ds(at, BLOCK)])
    for n, k in enumerate(ORDER):
        for m in range(4):
            at = pl.multiple_of(slab(j ^ m, k, x) * BLOCK, BLOCK)
            for r in range(4):
                rows = slice(r * BLOCK, (r + 1) * BLOCK)
                copy(parts[m].at[n, rows], a_s.at[pl.ds(at, BLOCK), rows])
    for cp in copies:
        cp.start()
    return copies[:16], copies[16:32], copies[32:]


def wait(copies):
    for cp in copies:
        cp.wait()


COPIES = 16 * 6


def norm_kernel(*refs):
    parts, out, a_s, g_s, doc_s, acc, starts, norms, sems = refs[:9], *refs[9:]
    docs, grads, acts = fetch(parts, a_s, g_s, doc_s, sems)
    a_s[SLABS * BLOCK :, :] = jnp.zeros((BLOCK, a_s.shape[1]), a_s.dtype)
    norms[...] = jnp.zeros_like(norms)
    wait(docs)
    doc = jnp.int32(-1)
    for t in range(SLABS):
        here = jnp.maximum(doc, jnp.max(doc_s[t].astype(jnp.float32)).astype(jnp.int32))
        new = here != doc

        @pl.when(new)
        def _(here=here, t=t):
            starts[here] = t

        doc = here
    starts[DOCS] = SLABS
    wait(grads)
    wait(acts)
    lane = lax.broadcasted_iota(jnp.int32, (1, BLOCK), 1)
    second = lax.broadcasted_iota(jnp.int32, (1, 2 * BLOCK), 1) >= BLOCK

    def product(first, end):
        at = pl.multiple_of(first * BLOCK, BLOCK)
        g = g_s[:, pl.ds(at, 2 * BLOCK)]
        g = jnp.where(jnp.logical_and(second, first + 1 >= end), jnp.zeros_like(g), g)
        return jnp.dot(g, a_s[pl.ds(at, 2 * BLOCK), :], preferred_element_type=jnp.float32)

    def squared(w, d):
        total = jnp.sum(jnp.sum(w * w, axis=0, keepdims=True), axis=1, keepdims=True)
        norms[...] = jnp.where(lane == d, total, norms[...])

    def document(d, carry):
        first, end = starts[d], starts[d + 1]

        @pl.when(end - first <= 2)
        def _():
            squared(product(first, end), d)

        @pl.when(end - first > 2)
        def _():
            acc[...] = product(first, end)

            def more(n, c):
                acc[...] = acc[...] + product(first + 2 * n, end)
                return c

            lax.fori_loop(1, (end - first + 1) // 2, more, 0)
            squared(acc[...], d)

        return carry

    lax.fori_loop(0, DOCS, document, 0)
    out[...] = jnp.broadcast_to(norms[...][None], out.shape)


def grad_kernel(*refs):
    norms, own, parts = refs[0], refs[1], refs[2:11]
    out, clip_out, a_s, g_s, doc_s, acc, sems = refs[11:]
    docs, grads, acts = fetch(parts, a_s, g_s, doc_s, sems)
    norm_sq = jnp.sum(norms[...], axis=0)
    clip = CLIP / jnp.sqrt(jnp.maximum(norm_sq, CLIP * CLIP))
    clip_out[...] = clip
    bound = jnp.sum(jnp.minimum(jnp.sqrt(own[0]), CLIP), axis=1, keepdims=True)
    shift = jnp.ceil(jnp.log2(jnp.maximum(bound, 1e-18))) - 14.0
    lane = lax.broadcasted_iota(jnp.int32, (1, BLOCK), 1).astype(jnp.float32)
    wait(docs)
    wait(grads)
    for t in range(SLABS):
        here = doc_s[t, 0:1, :].astype(jnp.float32) == lane
        factor = jnp.sum(jnp.where(here, clip, 0.0), axis=1, keepdims=True)
        g = g_s[:, t * BLOCK : (t + 1) * BLOCK].astype(jnp.float32)
        g_s[:, t * BLOCK : (t + 1) * BLOCK] = (g * factor).astype(jnp.bfloat16)
    tokens = SLABS * BLOCK
    wait(acts)
    acc[...] = jnp.dot(g_s[:, :tokens], a_s[:tokens, :], preferred_element_type=jnp.float32)
    scale = jnp.exp2(-shift)
    tail = jnp.broadcast_to(shift, (TAIL, BLOCK))
    for z in range(out.shape[0]):
        for y in range(4):
            piece = acc[z * COLS : (z + 1) * COLS, y * BLOCK : (y + 1) * BLOCK]
            out[z, y, :COLS] = piece * scale
            out[z, y, COLS:] = tail


def body(sizes, activations, out_grads, segment_ids):
    a, g, ids = activations[0], out_grads[0], segment_ids
    levels = sizes["zh"] * sizes["zl"]
    wide = levels * COLS
    bf16, f32 = jnp.bfloat16, jnp.float32
    vmem = pl.BlockSpec(memory_space=pltpu.VMEM)
    anywhere = pl.BlockSpec(memory_space=pl.ANY)

    payload = pl.pallas_call(
        prep_kernel,
        out_shape=[jax.ShapeDtypeStruct((wide + PART + PAD, BLOCK), bf16)] * 4,
        in_specs=[vmem, vmem, vmem],
        out_specs=[vmem] * 4,
        scratch_shapes=[pltpu.VMEM((g.shape[1], BLOCK), bf16)],
        interpret=INTERPRET,
        name="prep",
    )(ids, a, g)

    arrived = [
        lax.ppermute(payload[n], MOVE, table(sizes, MOVE, functools.partial(to_group, k)))
        for n, k in enumerate(ORDER)
    ]
    flip = [(0, 1), (1, 0)]
    last_g = jnp.stack([p[:wide] for p in arrived[2:]])
    last_g = lax.all_to_all(
        jnp.broadcast_to(last_g, (4, *last_g.shape)), "x", split_axis=0, concat_axis=0, tiled=True
    )
    own_a = jnp.stack([p[wide:] for p in arrived])
    own_g = jnp.stack([p[:wide] for p in arrived[:2]])
    partner = lax.ppermute(own_a, "yl", flip)
    own_other = lax.ppermute(own_a, "c", flip)
    g_parts = [own_g]
    for m in (1, 2, 3):
        g_parts.append(lax.ppermute(own_g, "x", [(s, (s + m) % 4) for s in range(4)]))
    partner_other = lax.ppermute(partner, "c", flip)
    a_parts = [own_a, own_other, partner, partner_other]
    parts = a_parts + g_parts + [last_g]

    stores = [
        pltpu.VMEM(((SLABS + 1) * BLOCK, PART), bf16),
        pltpu.VMEM((wide, (SLABS + 1) * BLOCK), bf16),
        pltpu.VMEM((SLABS, PAD, BLOCK), bf16),
        pltpu.VMEM((wide, PART), f32),
    ]
    sems = [pltpu.SemaphoreType.DMA((COPIES,))]
    row = jax.ShapeDtypeStruct((1, BLOCK), f32)
    partial = pl.pallas_call(
        norm_kernel,
        out_shape=jax.ShapeDtypeStruct((16, 1, BLOCK), f32),
        in_specs=[anywhere] * 9,
        out_specs=vmem,
        scratch_shapes=stores + [pltpu.SMEM((DOCS + 1,), jnp.int32), pltpu.VMEM((1, BLOCK), f32)] + sems,
        interpret=INTERPRET,
        name="norms",
    )(*parts)
    norms = lax.all_to_all(partial, GROUP, split_axis=0, concat_axis=0, tiled=True)
    pieces, clip = pl.pallas_call(
        grad_kernel,
        out_shape=[jax.ShapeDtypeStruct((levels, 4, COLS + TAIL, BLOCK), f32), row],
        in_specs=[vmem, vmem] + [anywhere] * 9,
        out_specs=[vmem] * 2,
        scratch_shapes=stores + sems,
        interpret=INTERPRET,
        name="grads",
    )(norms, partial, *parts)
    pieces = pieces.astype(jnp.float16).reshape(levels * 4, COLS + TAIL, BLOCK)
    summands = lax.all_to_all(pieces, SUMMED, split_axis=0, concat_axis=0, tiled=True).astype(f32)
    weight_grad = jnp.sum(summands[:, :COLS] * jnp.exp2(summands[:, COLS : COLS + 1]), axis=0).T
    home = [(dst, src) for src, dst in table(sizes, MOVE, functools.partial(to_group, 0))]
    clip = lax.ppermute(clip, MOVE, home)
    return weight_grad, clip[:, :DOCS]


def solution(mesh):
    heights = mesh.devices.size // 128
    dims = (heights, 2, 2, 2, 4, 4)
    fine = Mesh(mesh.devices.reshape(dims), AXES)
    dp, ctx = AXES[:4], AXES[4:]
    placed = (P(dp, ctx, None), P(dp, ctx, None), P(dp, ctx))
    return jax.shard_map(
        functools.partial(body, dict(zip(AXES, dims))),
        mesh=fine,
        in_specs=placed,
        out_specs=(P(ctx, dp), P(dp, None)),
        check_vma=False,
    )
```

```python
import functools

import jax
import jax.numpy as jnp
import numpy as np
from jax import lax
from jax.experimental import pallas as pl
from jax.experimental.pallas import tpu as pltpu
from jax.sharding import Mesh
from jax.sharding import PartitionSpec as P


INTERPRET = False
CLIP = 600.0
BLOCK = 128
COLS = 64
DOCS = 8
SLABS = 16
PART = 4 * BLOCK
TAIL = 8
PAD = 16

ORDER = (1, 3, 0, 2)
AXES = ("zh", "zl", "yl", "c", "yh", "x")
MOVE = ("yl", "c", "yh", "x")
GROUP = ("yl", "c", "x")
SUMMED = ("zh", "zl", "yh")


def table(sizes, axes, to):
    dims = [sizes[a] for a in axes]
    pairs = []
    for src in range(int(np.prod(dims))):
        at = dict(zip(axes, np.unravel_index(src, dims)))
        dst = to(**at)
        pairs.append((src, int(np.ravel_multi_index([int(dst[a]) for a in axes], dims))))
    return pairs


def to_group(k, yl, c, yh, x):
    j = yh ^ k
    return dict(yl=j // 2, c=j % 2, yh=c * 2 + yl, x=(x + k) % 4)


def prep_kernel(ids_ref, a_ref, g_ref, *rest):
    outs, gt_ref = rest[:4], rest[4]
    x, yh = lax.axis_index("x"), lax.axis_index("yh")
    chunks = g_ref.shape[1] // BLOCK
    ids = ids_ref[...]
    kept = ids >= 0
    doc = jnp.max(ids.astype(jnp.float32), axis=1, keepdims=True)
    doc = jnp.broadcast_to(doc, (PAD, BLOCK)).astype(jnp.bfloat16)
    for n in range(chunks):
        t = g_ref[:, n * BLOCK : (n + 1) * BLOCK].astype(jnp.float32).T
        gt_ref[n * BLOCK : (n + 1) * BLOCK, :] = jnp.where(kept, t, 0.0).astype(jnp.bfloat16)
    wide = chunks * BLOCK // 4
    for n, k in enumerate(ORDER):
        i = (x + k) % 4
        j = yh ^ k
        for z in range(wide // COLS):
            at = pl.multiple_of((z * 4 + j) * COLS, COLS)
            outs[n][z * COLS : (z + 1) * COLS, :] = gt_ref[pl.ds(at, COLS), :]
        for r in range(4):
            at = pl.multiple_of((r * 4 + i) * BLOCK, BLOCK)
            outs[n][wide + r * BLOCK : wide + (r + 1) * BLOCK, :] = a_ref[:, pl.ds(at, BLOCK)]
        outs[n][wide + PART :, :] = doc


def here():
    return lax.axis_index("x"), lax.axis_index("yl") * 2 + lax.axis_index("c")


def grads_of(parts, back, n, x):
    if n < 2:
        return parts[4 + back][n]
    return parts[8][(x + 4 - back) % 4, n - 2]


def features(slab):
    return jnp.concatenate([slab[r * BLOCK : (r + 1) * BLOCK] for r in range(4)], axis=1)


def number(slab):
    return slab[PART : PART + PAD].astype(jnp.float32)


def norm_kernel(*refs):
    parts, out, a_s, g_s, acc, starts, norms = refs[:9], *refs[9:]
    x, j = here()
    for n, k in enumerate(ORDER):
        for m in range(4):
            a_s[(j ^ (m ^ k)) * 4 + (x + 4 - k) % 4] = parts[m][n]
            g_s[(j ^ k) * 4 + (x + 8 - m - k) % 4] = grads_of(parts, m, n, x)
    a_s[SLABS] = jnp.zeros(a_s.shape[1:], a_s.dtype)
    norms[...] = jnp.zeros_like(norms)
    doc = jnp.int32(-1)
    for t in range(SLABS):
        this = jnp.maximum(doc, jnp.max(number(a_s[t])).astype(jnp.int32))

        @pl.when(this != doc)
        def _(this=this, t=t):
            starts[this] = t

        doc = this
    starts[DOCS] = SLABS
    lane = lax.broadcasted_iota(jnp.int32, (1, BLOCK), 1)
    second = lax.broadcasted_iota(jnp.int32, (1, 2 * BLOCK), 1) >= BLOCK

    def product(first, end):
        g = jnp.concatenate([g_s[first], g_s[first + 1]], axis=1)
        g = jnp.where(jnp.logical_and(second, first + 1 >= end), jnp.zeros_like(g), g)
        a = jnp.concatenate([features(a_s[first]), features(a_s[first + 1])], axis=0)
        return jnp.dot(g, a, preferred_element_type=jnp.float32)

    def squared(w, d):
        total = jnp.sum(jnp.sum(w * w, axis=0, keepdims=True), axis=1, keepdims=True)
        norms[...] = jnp.where(lane == d, total, norms[...])

    def document(d, carry):
        first, end = starts[d], starts[d + 1]

        @pl.when(end - first <= 2)
        def _():
            squared(product(first, end), d)

        @pl.when(end - first > 2)
        def _():
            acc[...] = product(first, end)

            def more(n, c):
                acc[...] = acc[...] + product(first + 2 * n, end)
                return c

            lax.fori_loop(1, (end - first + 1) // 2, more, 0)
            squared(acc[...], d)

        return carry

    lax.fori_loop(0, DOCS, document, 0)
    out[...] = jnp.broadcast_to(norms[...][None], out.shape)


def grad_kernel(*refs):
    norms, own, parts = refs[0], refs[1], refs[2:11]
    out, clip_out, g_s, acc = refs[11:]
    x, _ = here()
    norm_sq = jnp.sum(norms[...], axis=0)
    clip = CLIP / jnp.sqrt(jnp.maximum(norm_sq, CLIP * CLIP))
    clip_out[...] = clip
    bound = jnp.sum(jnp.minimum(jnp.sqrt(own[0]), CLIP), axis=1, keepdims=True)
    shift = jnp.ceil(jnp.log2(jnp.maximum(bound, 1e-18))) - 14.0
    lane = lax.broadcasted_iota(jnp.int32, (1, BLOCK), 1).astype(jnp.float32)
    acts = []
    for n, k in enumerate(ORDER):
        for m in range(4):
            a = parts[m][n]
            factor = jnp.sum(jnp.where(number(a)[0:1] == lane, clip, 0.0), axis=1, keepdims=True)
            g = grads_of(parts, (k - (m ^ k)) % 4, ORDER.index(m ^ k), x)
            g_s[len(acts)] = (g.astype(jnp.float32) * factor).astype(jnp.bfloat16)
            acts.append(features(a))
    acc[...] = jnp.dot(
        jnp.concatenate([g_s[t] for t in range(SLABS)], axis=1),
        jnp.concatenate(acts, axis=0),
        preferred_element_type=jnp.float32,
    )
    scale = jnp.exp2(-shift)
    tail = jnp.broadcast_to(shift, (TAIL, BLOCK))
    for z in range(out.shape[0]):
        for y in range(4):
            piece = acc[z * COLS : (z + 1) * COLS, y * BLOCK : (y + 1) * BLOCK]
            out[z, y, :COLS] = piece * scale
            out[z, y, COLS:] = tail


def body(sizes, activations, out_grads, segment_ids):
    a, g, ids = activations[0], out_grads[0], segment_ids
    levels = sizes["zh"] * sizes["zl"]
    wide = levels * COLS
    bf16, f32 = jnp.bfloat16, jnp.float32
    vmem = pl.BlockSpec(memory_space=pltpu.VMEM)
    small = pltpu.CompilerParams(vmem_limit_bytes=20 << 20)

    payload = pl.pallas_call(
        prep_kernel,
        out_shape=[jax.ShapeDtypeStruct((wide + PART + PAD, BLOCK), bf16)] * 4,
        in_specs=[vmem, vmem, vmem],
        out_specs=[vmem] * 4,
        scratch_shapes=[pltpu.VMEM((g.shape[1], BLOCK), bf16)],
        interpret=INTERPRET,
        compiler_params=small,
        name="prep",
    )(ids, a, g)

    arrived = [
        lax.ppermute(payload[n], MOVE, table(sizes, MOVE, functools.partial(to_group, k)))
        for n, k in enumerate(ORDER)
    ]
    flip = [(0, 1), (1, 0)]
    last_g = jnp.stack([p[:wide] for p in arrived[2:]])
    last_g = lax.all_to_all(
        jnp.broadcast_to(last_g, (4, *last_g.shape)), "x", split_axis=0, concat_axis=0, tiled=True
    )
    own_a = jnp.stack([p[wide:] for p in arrived])
    own_g = jnp.stack([p[:wide] for p in arrived[:2]])
    partner = lax.ppermute(own_a, "yl", flip)
    own_other = lax.ppermute(own_a, "c", flip)
    g_parts = [own_g]
    for m in (1, 2, 3):
        g_parts.append(lax.ppermute(own_g, "x", [(s, (s + m) % 4) for s in range(4)]))
    partner_other = lax.ppermute(partner, "c", flip)
    a_parts = [own_a, own_other, partner, partner_other]
    parts = a_parts + g_parts + [last_g]

    acts = pltpu.VMEM((SLABS + 1, PART + PAD, BLOCK), bf16)
    grads = pltpu.VMEM((SLABS + 1, wide, BLOCK), bf16)
    total = pltpu.VMEM((wide, PART), f32)
    starts = pltpu.SMEM((DOCS + 1,), jnp.int32)
    row = jax.ShapeDtypeStruct((1, BLOCK), f32)
    partial = pl.pallas_call(
        norm_kernel,
        out_shape=jax.ShapeDtypeStruct((16, 1, BLOCK), f32),
        in_specs=[vmem] * 9,
        out_specs=vmem,
        scratch_shapes=[acts, grads, total, starts, pltpu.VMEM((1, BLOCK), f32)],
        interpret=INTERPRET,
        compiler_params=small,
        name="norms",
    )(*parts)
    norms = lax.all_to_all(partial, GROUP, split_axis=0, concat_axis=0, tiled=True)
    pieces, clip = pl.pallas_call(
        grad_kernel,
        out_shape=[jax.ShapeDtypeStruct((levels, 4, COLS + TAIL, BLOCK), f32), row],
        in_specs=[vmem, vmem] + [vmem] * 9,
        out_specs=[vmem] * 2,
        scratch_shapes=[grads, total],
        interpret=INTERPRET,
        compiler_params=small,
        name="grads",
    )(norms, partial, *parts)
    pieces = pieces.astype(jnp.float16).reshape(levels * 4, COLS + TAIL, BLOCK)
    summands = lax.all_to_all(pieces, SUMMED, split_axis=0, concat_axis=0, tiled=True).astype(f32)
    weight_grad = jnp.sum(summands[:, :COLS] * jnp.exp2(summands[:, COLS : COLS + 1]), axis=0).T
    home = [(dst, src) for src, dst in table(sizes, MOVE, functools.partial(to_group, 0))]
    clip = lax.ppermute(clip, MOVE, home)
    return weight_grad, clip[:, :DOCS]


def solution(mesh):
    heights = mesh.devices.size // 128
    dims = (heights, 2, 2, 2, 4, 4)
    fine = Mesh(mesh.devices.reshape(dims), AXES)
    dp, ctx = AXES[:4], AXES[4:]
    placed = (P(dp, ctx, None), P(dp, ctx, None), P(dp, ctx))
    return jax.shard_map(
        functools.partial(body, dict(zip(AXES, dims))),
        mesh=fine,
        in_specs=placed,
        out_specs=(P(ctx, dp), P(dp, None)),
        check_vma=False,
    )
```

```python
import functools

import jax
import jax.numpy as jnp
import numpy as np
from jax import lax
from jax.experimental import pallas as pl
from jax.experimental.pallas import tpu as pltpu
from jax.sharding import Mesh
from jax.sharding import PartitionSpec as P


INTERPRET = False
HBM = pltpu.HBM
CLIP = 600.0
BLOCK = 128
COLS = 64
DOCS = 8
SLABS = 16
PART = 4 * BLOCK
TAIL = 8
PAD = 16

ORDER = (1, 3, 0, 2)
AXES = ("zh", "zl", "yl", "c", "yh", "x")
MOVE = ("yl", "c", "yh", "x")
GROUP = ("yl", "c", "x")
SUMMED = ("zh", "zl", "yh")


def table(sizes, axes, to):
    dims = [sizes[a] for a in axes]
    pairs = []
    for src in range(int(np.prod(dims))):
        at = dict(zip(axes, np.unravel_index(src, dims)))
        dst = to(**at)
        pairs.append((src, int(np.ravel_multi_index([int(dst[a]) for a in axes], dims))))
    return pairs


def to_group(k, yl, c, yh, x):
    j = yh ^ k
    return dict(yl=j // 2, c=j % 2, yh=c * 2 + yl, x=(x + k) % 4)


def prep_kernel(ids_in, a_in, g_in, *rest):
    outs, gt_ref, ids_ref, a_ref, g_ref, sems = rest[:4], *rest[4:]
    copies = [
        pltpu.make_async_copy(src, dst, sems.at[n])
        for n, (src, dst) in enumerate(((g_in, g_ref), (ids_in, ids_ref), (a_in, a_ref)))
    ]
    for cp in copies:
        cp.start()
    copies[0].wait()
    copies[1].wait()
    x, yh = lax.axis_index("x"), lax.axis_index("yh")
    chunks = g_ref.shape[1] // BLOCK
    ids = ids_ref[...]
    kept = ids >= 0
    doc = jnp.max(ids.astype(jnp.float32), axis=1, keepdims=True)
    doc = jnp.broadcast_to(doc, (PAD, BLOCK)).astype(jnp.bfloat16)
    for n in range(chunks):
        t = g_ref[:, n * BLOCK : (n + 1) * BLOCK].astype(jnp.float32).T
        gt_ref[n * BLOCK : (n + 1) * BLOCK, :] = jnp.where(kept, t, 0.0).astype(jnp.bfloat16)
    wide = chunks * BLOCK // 4
    copies[2].wait()
    for n, k in enumerate(ORDER):
        i = (x + k) % 4
        j = yh ^ k
        for z in range(wide // COLS):
            at = pl.multiple_of((z * 4 + j) * COLS, COLS)
            outs[n][z * COLS : (z + 1) * COLS, :] = gt_ref[pl.ds(at, COLS), :]
        for r in range(4):
            at = pl.multiple_of((r * 4 + i) * BLOCK, BLOCK)
            outs[n][wide + r * BLOCK : wide + (r + 1) * BLOCK, :] = a_ref[:, pl.ds(at, BLOCK)]
        outs[n][wide + PART :, :] = doc


def here():
    return lax.axis_index("x"), lax.axis_index("yl") * 2 + lax.axis_index("c")


def features(slab):
    return jnp.concatenate([slab[r * BLOCK : (r + 1) * BLOCK] for r in range(4)], axis=1)


def number(slab):
    return slab[PART : PART + PAD].astype(jnp.float32)


def norm_kernel(*refs):
    parts, out, a_s, g_s, acc, starts, norms, sems = refs[:9], *refs[9:]
    x, j = here()
    copies = []
    for n, k in enumerate(ORDER[2:]):
        for m in range(4):
            at = (j ^ k) * 4 + (m + 4 - k) % 4
            copies.append(pltpu.make_async_copy(parts[8].at[m, n], g_s.at[at], sems.at[len(copies)]))
    for cp in copies:
        cp.start()
    for n, k in enumerate(ORDER):
        for m in range(4):
            a_s[(j ^ (m ^ k)) * 4 + (x + 4 - k) % 4] = parts[m][n]
            if n < 2:
                g_s[(j ^ k) * 4 + (x + 8 - m - k) % 4] = parts[4 + m][n]
    a_s[SLABS] = jnp.zeros(a_s.shape[1:], a_s.dtype)
    norms[...] = jnp.zeros_like(norms)
    doc = jnp.int32(-1)
    for t in range(SLABS):
        this = jnp.maximum(doc, jnp.max(number(a_s[t])).astype(jnp.int32))

        @pl.when(this != doc)
        def _(this=this, t=t):
            starts[this] = t

        doc = this
    starts[DOCS] = SLABS
    for cp in copies:
        cp.wait()
    lane = lax.broadcasted_iota(jnp.int32, (1, BLOCK), 1)
    second = lax.broadcasted_iota(jnp.int32, (1, 2 * BLOCK), 1) >= BLOCK

    def product(first, end):
        g = jnp.concatenate([g_s[first], g_s[first + 1]], axis=1)
        g = jnp.where(jnp.logical_and(second, first + 1 >= end), jnp.zeros_like(g), g)
        a = jnp.concatenate([features(a_s[first]), features(a_s[first + 1])], axis=0)
        return jnp.dot(g, a, preferred_element_type=jnp.float32)

    def squared(w, d):
        total = jnp.sum(jnp.sum(w * w, axis=0, keepdims=True), axis=1, keepdims=True)
        norms[...] = jnp.where(lane == d, total, norms[...])

    def document(d, carry):
        first, end = starts[d], starts[d + 1]

        @pl.when(end - first <= 2)
        def _():
            squared(product(first, end), d)

        @pl.when(end - first > 2)
        def _():
            acc[...] = product(first, end)

            def more(n, c):
                acc[...] = acc[...] + product(first + 2 * n, end)
                return c

            lax.fori_loop(1, (end - first + 1) // 2, more, 0)
            squared(acc[...], d)

        return carry

    lax.fori_loop(0, DOCS, document, 0)
    out[...] = jnp.broadcast_to(norms[...][None], out.shape)


def grad_kernel(*refs):
    norms, own, parts = refs[0], refs[1], refs[2:11]
    out, clip_out, g_s, acc, late, sem = refs[11:]
    x, _ = here()
    copy = pltpu.make_async_copy(parts[8], late, sem)
    copy.start()
    norm_sq = jnp.sum(norms[...], axis=0)
    clip = CLIP / jnp.sqrt(jnp.maximum(norm_sq, CLIP * CLIP))
    clip_out[...] = clip[:, :DOCS]
    bound = jnp.sum(jnp.minimum(jnp.sqrt(own[0]), CLIP), axis=1, keepdims=True)
    shift = jnp.ceil(jnp.log2(jnp.maximum(bound, 1e-18))) - 14.0
    lane = lax.broadcasted_iota(jnp.int32, (1, BLOCK), 1).astype(jnp.float32)
    acts = []
    for half in range(2):
        if half:
            copy.wait()
        for n, k in enumerate(ORDER):
            for m in range(4):
                kg = m ^ k
                ng, back = ORDER.index(kg), (k - kg) % 4
                if (ng >= 2) != half:
                    continue
                a = parts[m][n]
                g = late[(x + 4 - back) % 4, ng - 2] if half else parts[4 + back][ng]
                factor = jnp.sum(jnp.where(number(a)[0:1] == lane, clip, 0.0), axis=1, keepdims=True)
                g_s[len(acts)] = (g.astype(jnp.float32) * factor).astype(jnp.bfloat16)
                acts.append(features(a))
    acc[...] = jnp.dot(
        jnp.concatenate([g_s[t] for t in range(SLABS)], axis=1),
        jnp.concatenate(acts, axis=0),
        preferred_element_type=jnp.float32,
    )
    scale = jnp.exp2(-shift)
    tail = jnp.broadcast_to(shift, (TAIL, BLOCK))
    for z in range(out.shape[0]):
        for y in range(4):
            piece = acc[z * COLS : (z + 1) * COLS, y * BLOCK : (y + 1) * BLOCK]
            out[z, y, :COLS] = piece * scale
            out[z, y, COLS:] = tail


def hbm(p):
    return p if INTERPRET else pltpu.with_memory_space_constraint(p, HBM)


def body(sizes, activations, out_grads, segment_ids):
    a, g, ids = activations[0], out_grads[0], segment_ids
    levels = sizes["zh"] * sizes["zl"]
    wide = levels * COLS
    bf16, f32 = jnp.bfloat16, jnp.float32
    vmem = pl.BlockSpec(memory_space=pltpu.VMEM)
    anywhere = pl.BlockSpec(memory_space=HBM)
    small = pltpu.CompilerParams(vmem_limit_bytes=20 << 20)

    payload = pl.pallas_call(
        prep_kernel,
        out_shape=[jax.ShapeDtypeStruct((wide + PART + PAD, BLOCK), bf16)] * 4,
        in_specs=[anywhere] * 3,
        out_specs=[vmem] * 4,
        scratch_shapes=[
            pltpu.VMEM((g.shape[1], BLOCK), bf16),
            pltpu.VMEM(ids.shape, ids.dtype),
            pltpu.VMEM(a.shape, bf16),
            pltpu.VMEM(g.shape, bf16),
            pltpu.SemaphoreType.DMA((3,)),
        ],
        interpret=INTERPRET,
        compiler_params=small,
        name="prep",
    )(*[hbm(p) for p in (ids, a, g)])

    arrived = [
        lax.ppermute(payload[n], MOVE, table(sizes, MOVE, functools.partial(to_group, k)))
        for n, k in enumerate(ORDER)
    ]
    flip = [(0, 1), (1, 0)]
    last_g = jnp.stack([p[:wide] for p in arrived[2:]])
    last_g = lax.all_to_all(
        jnp.broadcast_to(last_g, (4, *last_g.shape)), "x", split_axis=0, concat_axis=0, tiled=True
    )
    own_a = jnp.stack([p[wide:] for p in arrived])
    own_g = jnp.stack([p[:wide] for p in arrived[:2]])
    partner = lax.ppermute(own_a, "yl", flip)
    own_other = lax.ppermute(own_a, "c", flip)
    g_parts = [own_g]
    for m in (1, 2, 3):
        g_parts.append(lax.ppermute(own_g, "x", [(s, (s + m) % 4) for s in range(4)]))
    partner_other = lax.ppermute(partner, "c", flip)
    a_parts = [own_a, own_other, partner, partner_other]
    parts = a_parts + g_parts + [hbm(last_g)]

    acts = pltpu.VMEM((SLABS + 1, PART + PAD, BLOCK), bf16)
    grads = pltpu.VMEM((SLABS + 1, wide, BLOCK), bf16)
    total = pltpu.VMEM((wide, PART), f32)
    starts = pltpu.SMEM((DOCS + 1,), jnp.int32)
    row = jax.ShapeDtypeStruct((1, DOCS), f32)
    partial = pl.pallas_call(
        norm_kernel,
        out_shape=jax.ShapeDtypeStruct((16, 1, BLOCK), f32),
        in_specs=[vmem] * 8 + [anywhere],
        out_specs=vmem,
        scratch_shapes=[acts, grads, total, starts, pltpu.VMEM((1, BLOCK), f32), pltpu.SemaphoreType.DMA((8,))],
        interpret=INTERPRET,
        compiler_params=small,
        name="norms",
    )(*parts)
    norms = lax.all_to_all(partial, GROUP, split_axis=0, concat_axis=0, tiled=True)
    pieces, clip = pl.pallas_call(
        grad_kernel,
        out_shape=[jax.ShapeDtypeStruct((levels, 4, COLS + TAIL, BLOCK), f32), row],
        in_specs=[vmem] * 10 + [anywhere],
        out_specs=[vmem] * 2,
        scratch_shapes=[grads, total, pltpu.VMEM(last_g.shape, bf16), pltpu.SemaphoreType.DMA],
        interpret=INTERPRET,
        compiler_params=small,
        name="grads",
    )(norms, partial, *parts)
    pieces = pieces.astype(jnp.float16).reshape(levels * 4, COLS + TAIL, BLOCK)
    summands = lax.all_to_all(pieces, SUMMED, split_axis=0, concat_axis=0, tiled=True).astype(f32)
    weight_grad = jnp.sum(summands[:, :COLS] * jnp.exp2(summands[:, COLS : COLS + 1]), axis=0).T
    home = [(dst, src) for src, dst in table(sizes, MOVE, functools.partial(to_group, 0))]
    clip = lax.ppermute(clip, MOVE, home)
    return weight_grad, clip


def solution(mesh):
    heights = mesh.devices.size // 128
    dims = (heights, 2, 2, 2, 4, 4)
    fine = Mesh(mesh.devices.reshape(dims), AXES)
    dp, ctx = AXES[:4], AXES[4:]
    placed = (P(dp, ctx, None), P(dp, ctx, None), P(dp, ctx))
    return jax.shard_map(
        functools.partial(body, dict(zip(AXES, dims))),
        mesh=fine,
        in_specs=placed,
        out_specs=(P(ctx, dp), P(dp, None)),
        check_vma=False,
    )
```

```python
import functools

import jax
import jax.numpy as jnp
import numpy as np
from jax import lax
from jax.experimental import pallas as pl
from jax.experimental.pallas import tpu as pltpu
from jax.sharding import Mesh
from jax.sharding import PartitionSpec as P


INTERPRET = False
HBM = pltpu.HBM
CLIP = 600.0
BLOCK = 128
COLS = 64
DOCS = 8
SLABS = 16
PART = 4 * BLOCK
TAIL = 8
PAD = 16

ORDER = (1, 3, 0, 2)
AXES = ("zh", "zl", "yl", "c", "yh", "x")
MOVE = ("yl", "c", "yh", "x")
GROUP = ("yl", "c", "x")
LEVELS = ("zh", "zl")


def table(sizes, axes, to):
    dims = [sizes[a] for a in axes]
    pairs = []
    for src in range(int(np.prod(dims))):
        at = dict(zip(axes, np.unravel_index(src, dims)))
        dst = to(**at)
        pairs.append((src, int(np.ravel_multi_index([int(dst[a]) for a in axes], dims))))
    return pairs


def to_group(k, yl, c, yh, x):
    j = yh ^ k
    return dict(yl=j // 2, c=j % 2, yh=c * 2 + yl, x=(x + k) % 4)


def prep_kernel(ids_in, a_in, g_in, *rest):
    outs, gt_ref, ids_ref, a_ref, g_ref, sems = rest[:4], *rest[4:]
    copies = [
        pltpu.make_async_copy(src, dst, sems.at[n])
        for n, (src, dst) in enumerate(((g_in, g_ref), (ids_in, ids_ref), (a_in, a_ref)))
    ]
    for cp in copies:
        cp.start()
    copies[0].wait()
    copies[1].wait()
    x, yh = lax.axis_index("x"), lax.axis_index("yh")
    chunks = g_ref.shape[1] // BLOCK
    ids = ids_ref[...]
    kept = ids >= 0
    doc = jnp.max(ids.astype(jnp.float32), axis=1, keepdims=True)
    doc = jnp.broadcast_to(doc, (PAD, BLOCK)).astype(jnp.bfloat16)
    for n in range(chunks):
        t = g_ref[:, n * BLOCK : (n + 1) * BLOCK].astype(jnp.float32).T
        gt_ref[n * BLOCK : (n + 1) * BLOCK, :] = jnp.where(kept, t, 0.0).astype(jnp.bfloat16)
    wide = chunks * BLOCK // 4
    copies[2].wait()
    for n, k in enumerate(ORDER):
        i = (x + k) % 4
        j = yh ^ k
        for z in range(wide // COLS):
            at = pl.multiple_of((z * 4 + j) * COLS, COLS)
            outs[n][z * COLS : (z + 1) * COLS, :] = gt_ref[pl.ds(at, COLS), :]
        for r in range(4):
            at = pl.multiple_of((r * 4 + i) * BLOCK, BLOCK)
            outs[n][wide + r * BLOCK : wide + (r + 1) * BLOCK, :] = a_ref[:, pl.ds(at, BLOCK)]
        outs[n][wide + PART :, :] = doc


def here():
    return lax.axis_index("x"), lax.axis_index("yl") * 2 + lax.axis_index("c")


def features(slab):
    return jnp.concatenate([slab[r * BLOCK : (r + 1) * BLOCK] for r in range(4)], axis=1)


def number(slab):
    return slab[PART : PART + PAD].astype(jnp.float32)


def norm_kernel(*refs):
    parts, out, a_s, g_s, acc, starts, norms, sems = refs[:9], *refs[9:]
    x, j = here()
    copies = []
    for n, k in enumerate(ORDER[2:]):
        for m in range(4):
            at = (j ^ k) * 4 + (m + 4 - k) % 4
            copies.append(pltpu.make_async_copy(parts[8].at[m, n], g_s.at[at], sems.at[len(copies)]))
    for cp in copies:
        cp.start()
    for n, k in enumerate(ORDER):
        for m in range(4):
            a_s[(j ^ (m ^ k)) * 4 + (x + 4 - k) % 4] = parts[m][n]
            if n < 2:
                g_s[(j ^ k) * 4 + (x + 8 - m - k) % 4] = parts[4 + m][n]
    a_s[SLABS] = jnp.zeros(a_s.shape[1:], a_s.dtype)
    norms[...] = jnp.zeros_like(norms)
    doc = jnp.int32(-1)
    for t in range(SLABS):
        this = jnp.maximum(doc, jnp.max(number(a_s[t])).astype(jnp.int32))

        @pl.when(this != doc)
        def _(this=this, t=t):
            starts[this] = t

        doc = this
    starts[DOCS] = SLABS
    for cp in copies:
        cp.wait()
    lane = lax.broadcasted_iota(jnp.int32, (1, BLOCK), 1)
    second = lax.broadcasted_iota(jnp.int32, (1, 2 * BLOCK), 1) >= BLOCK

    def product(first, end):
        g = jnp.concatenate([g_s[first], g_s[first + 1]], axis=1)
        g = jnp.where(jnp.logical_and(second, first + 1 >= end), jnp.zeros_like(g), g)
        a = jnp.concatenate([features(a_s[first]), features(a_s[first + 1])], axis=0)
        return jnp.dot(g, a, preferred_element_type=jnp.float32)

    def squared(w, d):
        total = jnp.sum(jnp.sum(w * w, axis=0, keepdims=True), axis=1, keepdims=True)
        norms[...] = jnp.where(lane == d, total, norms[...])

    def document(d, carry):
        first, end = starts[d], starts[d + 1]

        @pl.when(end - first <= 2)
        def _():
            squared(product(first, end), d)

        @pl.when(end - first > 2)
        def _():
            acc[...] = product(first, end)

            def more(n, c):
                acc[...] = acc[...] + product(first + 2 * n, end)
                return c

            lax.fori_loop(1, (end - first + 1) // 2, more, 0)
            squared(acc[...], d)

        return carry

    lax.fori_loop(0, DOCS, document, 0)
    out[...] = jnp.broadcast_to(norms[...][None], out.shape)


def grad_kernel(*refs):
    norms, own, parts = refs[0], refs[1], refs[2:11]
    out, clip_out, g_s, acc, late, sem = refs[11:]
    x, _ = here()
    copy = pltpu.make_async_copy(parts[8], late, sem)
    copy.start()
    norm_sq = jnp.sum(norms[...], axis=0)
    clip = CLIP / jnp.sqrt(jnp.maximum(norm_sq, CLIP * CLIP))
    clip_out[...] = clip[:, :DOCS]
    bound = jnp.sum(jnp.minimum(jnp.sqrt(own[0]), CLIP), axis=1, keepdims=True)
    shift = jnp.ceil(jnp.log2(jnp.maximum(bound, 1e-18))) - 14.0
    lane = lax.broadcasted_iota(jnp.int32, (1, BLOCK), 1).astype(jnp.float32)
    acts = []
    for half in range(2):
        if half:
            copy.wait()
        for n, k in enumerate(ORDER):
            for m in range(4):
                kg = m ^ k
                ng, back = ORDER.index(kg), (k - kg) % 4
                if (ng >= 2) != half:
                    continue
                a = parts[m][n]
                g = late[(x + 4 - back) % 4, ng - 2] if half else parts[4 + back][ng]
                factor = jnp.sum(jnp.where(number(a)[0:1] == lane, clip, 0.0), axis=1, keepdims=True)
                g_s[len(acts)] = (g.astype(jnp.float32) * factor).astype(jnp.bfloat16)
                acts.append(features(a))
    acc[...] = jnp.dot(
        jnp.concatenate([g_s[t] for t in range(SLABS)], axis=1),
        jnp.concatenate(acts, axis=0),
        preferred_element_type=jnp.float32,
    )
    scale = jnp.exp2(-shift)
    tail = jnp.broadcast_to(shift, (TAIL, BLOCK))
    for z in range(out.shape[0]):
        for y in range(4):
            piece = acc[z * COLS : (z + 1) * COLS, y * BLOCK : (y + 1) * BLOCK]
            out[z, y, :COLS] = piece * scale
            out[z, y, COLS:] = tail


def hbm(p):
    return p if INTERPRET else pltpu.with_memory_space_constraint(p, HBM)


def body(sizes, activations, out_grads, segment_ids):
    a, g, ids = activations[0], out_grads[0], segment_ids
    levels = sizes["zh"] * sizes["zl"]
    wide = levels * COLS
    bf16, f32 = jnp.bfloat16, jnp.float32
    vmem = pl.BlockSpec(memory_space=pltpu.VMEM)
    anywhere = pl.BlockSpec(memory_space=HBM)
    small = pltpu.CompilerParams(vmem_limit_bytes=20 << 20)

    payload = pl.pallas_call(
        prep_kernel,
        out_shape=[jax.ShapeDtypeStruct((wide + PART + PAD, BLOCK), bf16)] * 4,
        in_specs=[anywhere] * 3,
        out_specs=[vmem] * 4,
        scratch_shapes=[
            pltpu.VMEM((g.shape[1], BLOCK), bf16),
            pltpu.VMEM(ids.shape, ids.dtype),
            pltpu.VMEM(a.shape, bf16),
            pltpu.VMEM(g.shape, bf16),
            pltpu.SemaphoreType.DMA((3,)),
        ],
        interpret=INTERPRET,
        compiler_params=small,
        name="prep",
    )(*[hbm(p) for p in (ids, a, g)])

    arrived = [
        lax.ppermute(payload[n], MOVE, table(sizes, MOVE, functools.partial(to_group, k)))
        for n, k in enumerate(ORDER)
    ]
    flip = [(0, 1), (1, 0)]
    last_g = jnp.stack([p[:wide] for p in arrived[2:]])
    last_g = lax.all_to_all(
        jnp.broadcast_to(last_g, (4, *last_g.shape)), "x", split_axis=0, concat_axis=0, tiled=True
    )
    own_a = jnp.stack([p[wide:] for p in arrived])
    own_g = jnp.stack([p[:wide] for p in arrived[:2]])
    partner = lax.ppermute(own_a, "yl", flip)
    own_other = lax.ppermute(own_a, "c", flip)
    g_parts = [own_g]
    for m in (1, 2, 3):
        g_parts.append(lax.ppermute(own_g, "x", [(s, (s + m) % 4) for s in range(4)]))
    partner_other = lax.ppermute(partner, "c", flip)
    a_parts = [own_a, own_other, partner, partner_other]
    parts = a_parts + g_parts + [hbm(last_g)]

    acts = pltpu.VMEM((SLABS + 1, PART + PAD, BLOCK), bf16)
    grads = pltpu.VMEM((SLABS + 1, wide, BLOCK), bf16)
    total = pltpu.VMEM((wide, PART), f32)
    starts = pltpu.SMEM((DOCS + 1,), jnp.int32)
    row = jax.ShapeDtypeStruct((1, DOCS), f32)
    partial = pl.pallas_call(
        norm_kernel,
        out_shape=jax.ShapeDtypeStruct((16, 1, BLOCK), f32),
        in_specs=[vmem] * 8 + [anywhere],
        out_specs=vmem,
        scratch_shapes=[acts, grads, total, starts, pltpu.VMEM((1, BLOCK), f32), pltpu.SemaphoreType.DMA((8,))],
        interpret=INTERPRET,
        compiler_params=small,
        name="norms",
    )(*parts)
    norms = lax.all_to_all(partial, GROUP, split_axis=0, concat_axis=0, tiled=True)
    pieces, clip = pl.pallas_call(
        grad_kernel,
        out_shape=[jax.ShapeDtypeStruct((levels, 4, COLS + TAIL, BLOCK), f32), row],
        in_specs=[vmem] * 10 + [anywhere],
        out_specs=[vmem] * 2,
        scratch_shapes=[grads, total, pltpu.VMEM(last_g.shape, bf16), pltpu.SemaphoreType.DMA],
        interpret=INTERPRET,
        compiler_params=small,
        name="grads",
    )(norms, partial, *parts)
    pieces = pieces.astype(jnp.float16)
    shares = lax.all_to_all(pieces, LEVELS, split_axis=0, concat_axis=0, tiled=True).astype(f32)
    shares = jnp.sum(shares[:, :, :COLS] * jnp.exp2(shares[:, :, COLS : COLS + 1]), axis=0)
    summands = lax.all_to_all(shares, "yh", split_axis=0, concat_axis=0, tiled=True)
    weight_grad = jnp.sum(summands, axis=0).T
    home = [(dst, src) for src, dst in table(sizes, MOVE, functools.partial(to_group, 0))]
    clip = lax.ppermute(clip, MOVE, home)
    return weight_grad, clip


def solution(mesh):
    heights = mesh.devices.size // 128
    dims = (heights, 2, 2, 2, 4, 4)
    fine = Mesh(mesh.devices.reshape(dims), AXES)
    dp, ctx = AXES[:4], AXES[4:]
    placed = (P(dp, ctx, None), P(dp, ctx, None), P(dp, ctx))
    return jax.shard_map(
        functools.partial(body, dict(zip(AXES, dims))),
        mesh=fine,
        in_specs=placed,
        out_specs=(P(ctx, dp), P(dp, None)),
        check_vma=False,
    )
```

```python
import functools

import jax
import jax.numpy as jnp
import numpy as np
from jax import lax
from jax.experimental import pallas as pl
from jax.experimental.pallas import tpu as pltpu
from jax.sharding import Mesh
from jax.sharding import PartitionSpec as P


INTERPRET = False
HBM = pltpu.HBM
CLIP = 600.0
BLOCK = 128
COLS = 64
DOCS = 8
SLABS = 16
PART = 4 * BLOCK
TAIL = 8
PAD = 16

ORDER = (1, 3, 0, 2)
AXES = ("zh", "zl", "yl", "c", "yh", "x")
MOVE = ("yl", "c", "yh", "x")
GROUP = ("yl", "c", "x")
SUMMED = ("yh", "zh", "zl")


def table(sizes, axes, to):
    dims = [sizes[a] for a in axes]
    pairs = []
    for src in range(int(np.prod(dims))):
        at = dict(zip(axes, np.unravel_index(src, dims)))
        dst = to(**at)
        pairs.append((src, int(np.ravel_multi_index([int(dst[a]) for a in axes], dims))))
    return pairs


def to_group(k, yl, c, yh, x):
    j = yh ^ k
    return dict(yl=j // 2, c=j % 2, yh=c * 2 + yl, x=(x + k) % 4)


def prep_kernel(ids_in, a_in, g_in, *rest):
    outs, gt_ref, ids_ref, a_ref, g_ref, sems = rest[:4], *rest[4:]
    copies = [
        pltpu.make_async_copy(src, dst, sems.at[n])
        for n, (src, dst) in enumerate(((g_in, g_ref), (ids_in, ids_ref), (a_in, a_ref)))
    ]
    for cp in copies:
        cp.start()
    copies[0].wait()
    copies[1].wait()
    x, yh = lax.axis_index("x"), lax.axis_index("yh")
    chunks = g_ref.shape[1] // BLOCK
    ids = ids_ref[...]
    kept = ids >= 0
    doc = jnp.max(ids.astype(jnp.float32), axis=1, keepdims=True)
    doc = jnp.broadcast_to(doc, (PAD, BLOCK)).astype(jnp.bfloat16)
    for n in range(chunks):
        t = g_ref[:, n * BLOCK : (n + 1) * BLOCK].astype(jnp.float32).T
        gt_ref[n * BLOCK : (n + 1) * BLOCK, :] = jnp.where(kept, t, 0.0).astype(jnp.bfloat16)
    wide = chunks * BLOCK // 4
    copies[2].wait()
    for n, k in enumerate(ORDER):
        i = (x + k) % 4
        j = yh ^ k
        for z in range(wide // COLS):
            at = pl.multiple_of((z * 4 + j) * COLS, COLS)
            outs[n][z * COLS : (z + 1) * COLS, :] = gt_ref[pl.ds(at, COLS), :]
        for r in range(4):
            at = pl.multiple_of((r * 4 + i) * BLOCK, BLOCK)
            outs[n][wide + r * BLOCK : wide + (r + 1) * BLOCK, :] = a_ref[:, pl.ds(at, BLOCK)]
        outs[n][wide + PART :, :] = doc


def here():
    return lax.axis_index("x"), lax.axis_index("yl") * 2 + lax.axis_index("c")


def features(slab):
    return jnp.concatenate([slab[r * BLOCK : (r + 1) * BLOCK] for r in range(4)], axis=1)


def number(slab):
    return slab[PART : PART + PAD].astype(jnp.float32)


def norm_kernel(*refs):
    parts, out, a_s, g_s, acc, starts, numbers, norms, sems = refs[:9], *refs[9:]
    x, j = here()
    copies = []
    for n, k in enumerate(ORDER[2:]):
        for m in range(4):
            at = (j ^ k) * 4 + (m + 4 - k) % 4
            copies.append(pltpu.make_async_copy(parts[8].at[m, n], g_s.at[at], sems.at[len(copies)]))
    for cp in copies:
        cp.start()
    for n, k in enumerate(ORDER):
        for m in range(4):
            t = (j ^ (m ^ k)) * 4 + (x + 4 - k) % 4
            a_s[t] = parts[m][n]
            numbers[t] = jnp.max(number(parts[m][n])[0:1]).astype(jnp.int32)
            if n < 2:
                g_s[(j ^ k) * 4 + (x + 8 - m - k) % 4] = parts[4 + m][n]
    a_s[SLABS] = jnp.zeros(a_s.shape[1:], a_s.dtype)
    norms[...] = jnp.zeros_like(norms)
    reached, doc = [], jnp.int32(0)
    for t in range(SLABS):
        doc = jnp.maximum(doc, numbers[t])
        reached.append(doc)
    for t in reversed(range(SLABS)):
        starts[reached[t]] = t
    starts[DOCS] = SLABS
    for cp in copies:
        cp.wait()
    lane = lax.broadcasted_iota(jnp.int32, (1, BLOCK), 1)
    second = lax.broadcasted_iota(jnp.int32, (1, 2 * BLOCK), 1) >= BLOCK

    def product(first, end):
        g = jnp.concatenate([g_s[first], g_s[first + 1]], axis=1)
        g = jnp.where(jnp.logical_and(second, first + 1 >= end), jnp.zeros_like(g), g)
        a = jnp.concatenate([features(a_s[first]), features(a_s[first + 1])], axis=0)
        return jnp.dot(g, a, preferred_element_type=jnp.float32)

    def squared(w, d):
        total = jnp.sum(jnp.sum(w * w, axis=0, keepdims=True), axis=1, keepdims=True)
        norms[...] = jnp.where(lane == d, total, norms[...])

    def document(d, carry):
        first, end = starts[d], starts[d + 1]

        @pl.when(end - first <= 2)
        def _():
            squared(product(first, end), d)

        @pl.when(end - first > 2)
        def _():
            acc[...] = product(first, end)

            def more(n, c):
                acc[...] = acc[...] + product(first + 2 * n, end)
                return c

            lax.fori_loop(1, (end - first + 1) // 2, more, 0)
            squared(acc[...], d)

        return carry

    lax.fori_loop(0, DOCS, document, 0)
    out[...] = jnp.broadcast_to(norms[...][None], out.shape)


def grad_kernel(*refs):
    norms, own, parts = refs[0], refs[1], refs[2:11]
    out, clip_out, g_s, acc, late, sem = refs[11:]
    x, _ = here()
    copy = pltpu.make_async_copy(parts[8], late, sem)
    copy.start()
    norm_sq = jnp.sum(norms[...], axis=0)
    clip = CLIP / jnp.sqrt(jnp.maximum(norm_sq, CLIP * CLIP))
    clip_out[...] = clip[:, :DOCS]
    bound = jnp.sum(jnp.minimum(jnp.sqrt(own[0]), CLIP), axis=1, keepdims=True)
    shift = jnp.ceil(jnp.log2(jnp.maximum(bound, 1e-18))) - 14.0
    lane = lax.broadcasted_iota(jnp.int32, (1, BLOCK), 1).astype(jnp.float32)
    acts = []
    for half in range(2):
        if half:
            copy.wait()
        for n, k in enumerate(ORDER):
            for m in range(4):
                kg = m ^ k
                ng, back = ORDER.index(kg), (k - kg) % 4
                if (ng >= 2) != half:
                    continue
                a = parts[m][n]
                g = late[(x + 4 - back) % 4, ng - 2] if half else parts[4 + back][ng]
                factor = jnp.sum(jnp.where(number(a)[0:1] == lane, clip, 0.0), axis=1, keepdims=True)
                g_s[len(acts)] = (g.astype(jnp.float32) * factor).astype(jnp.bfloat16)
                acts.append(features(a))
    acc[...] = jnp.dot(
        jnp.concatenate([g_s[t] for t in range(SLABS)], axis=1),
        jnp.concatenate(acts, axis=0),
        preferred_element_type=jnp.float32,
    )
    scale = jnp.exp2(-shift)
    tail = jnp.broadcast_to(shift, (TAIL, BLOCK))
    for z in range(out.shape[1]):
        for y in range(4):
            piece = acc[z * COLS : (z + 1) * COLS, y * BLOCK : (y + 1) * BLOCK]
            out[y, z, :COLS] = piece * scale
            out[y, z, COLS:] = tail


def hbm(p):
    return p if INTERPRET else pltpu.with_memory_space_constraint(p, HBM)


def body(sizes, activations, out_grads, segment_ids):
    a, g, ids = activations[0], out_grads[0], segment_ids
    levels = sizes["zh"] * sizes["zl"]
    wide = levels * COLS
    bf16, f32 = jnp.bfloat16, jnp.float32
    vmem = pl.BlockSpec(memory_space=pltpu.VMEM)
    anywhere = pl.BlockSpec(memory_space=HBM)
    small = pltpu.CompilerParams(vmem_limit_bytes=20 << 20)

    payload = pl.pallas_call(
        prep_kernel,
        out_shape=[jax.ShapeDtypeStruct((wide + PART + PAD, BLOCK), bf16)] * 4,
        in_specs=[anywhere] * 3,
        out_specs=[vmem] * 4,
        scratch_shapes=[
            pltpu.VMEM((g.shape[1], BLOCK), bf16),
            pltpu.VMEM(ids.shape, ids.dtype),
            pltpu.VMEM(a.shape, bf16),
            pltpu.VMEM(g.shape, bf16),
            pltpu.SemaphoreType.DMA((3,)),
        ],
        interpret=INTERPRET,
        compiler_params=small,
        name="prep",
    )(*[hbm(p) for p in (ids, a, g)])

    arrived = [
        lax.ppermute(payload[n], MOVE, table(sizes, MOVE, functools.partial(to_group, k)))
        for n, k in enumerate(ORDER)
    ]
    flip = [(0, 1), (1, 0)]
    last_g = jnp.stack([p[:wide] for p in arrived[2:]])
    last_g = lax.all_to_all(
        jnp.broadcast_to(last_g, (4, *last_g.shape)), "x", split_axis=0, concat_axis=0, tiled=True
    )
    own_a = jnp.stack([p[wide:] for p in arrived])
    own_g = jnp.stack([p[:wide] for p in arrived[:2]])
    partner = lax.ppermute(own_a, "yl", flip)
    own_other = lax.ppermute(own_a, "c", flip)
    g_parts = [own_g]
    for m in (1, 2, 3):
        g_parts.append(lax.ppermute(own_g, "x", [(s, (s + m) % 4) for s in range(4)]))
    partner_other = lax.ppermute(partner, "c", flip)
    a_parts = [own_a, own_other, partner, partner_other]
    parts = a_parts + g_parts + [hbm(last_g)]

    acts = pltpu.VMEM((SLABS + 1, PART + PAD, BLOCK), bf16)
    grads = pltpu.VMEM((SLABS + 1, wide, BLOCK), bf16)
    total = pltpu.VMEM((wide, PART), f32)
    starts = pltpu.SMEM((DOCS + 1,), jnp.int32)
    row = jax.ShapeDtypeStruct((1, DOCS), f32)
    partial = pl.pallas_call(
        norm_kernel,
        out_shape=jax.ShapeDtypeStruct((16, 1, BLOCK), f32),
        in_specs=[vmem] * 8 + [anywhere],
        out_specs=vmem,
        scratch_shapes=[acts, grads, total, starts, pltpu.SMEM((SLABS,), jnp.int32), pltpu.VMEM((1, BLOCK), f32), pltpu.SemaphoreType.DMA((8,))],
        interpret=INTERPRET,
        compiler_params=small,
        name="norms",
    )(*parts)
    norms = lax.all_to_all(partial, GROUP, split_axis=0, concat_axis=0, tiled=True)
    pieces, clip = pl.pallas_call(
        grad_kernel,
        out_shape=[jax.ShapeDtypeStruct((4, levels, COLS + TAIL, BLOCK), f32), row],
        in_specs=[vmem] * 10 + [anywhere],
        out_specs=[vmem] * 2,
        scratch_shapes=[grads, total, pltpu.VMEM(last_g.shape, bf16), pltpu.SemaphoreType.DMA],
        interpret=INTERPRET,
        compiler_params=small,
        name="grads",
    )(norms, partial, *parts)
    pieces = pieces.astype(jnp.float16).reshape(levels * 4, COLS + TAIL, BLOCK)
    summands = lax.all_to_all(pieces, SUMMED, split_axis=0, concat_axis=0, tiled=True).astype(f32)
    weight_grad = jnp.sum(summands[:, :COLS] * jnp.exp2(summands[:, COLS : COLS + 1]), axis=0).T
    home = [(dst, src) for src, dst in table(sizes, MOVE, functools.partial(to_group, 0))]
    clip = lax.ppermute(clip, MOVE, home)
    return weight_grad, clip


def solution(mesh):
    heights = mesh.devices.size // 128
    dims = (heights, 2, 2, 2, 4, 4)
    fine = Mesh(mesh.devices.reshape(dims), AXES)
    dp, ctx = AXES[:4], AXES[4:]
    placed = (P(dp, ctx, None), P(dp, ctx, None), P(dp, ctx))
    return jax.shard_map(
        functools.partial(body, dict(zip(AXES, dims))),
        mesh=fine,
        in_specs=placed,
        out_specs=(P(ctx, dp), P(dp, None)),
        check_vma=False,
    )
```
